256 devices in a mesh: cluster: 8 (over z), sub: 32 (over x, y, core).
Axes of the slice: x: 4, y: 4, z: 8, core: 2. Of those that a mesh axis runs over, the one named last changes fastest.
Arguments:
- dual_ops: bfloat16 [8, 32, 2048, 2048], P('cluster', 'sub'), as said below
- corner_coupling: float32 [8, 32, 48, 2048], P('cluster', 'sub'), may hold values from -0.3 to 0.3
- coarse_inverse: float32 [32, 128, 128], P('sub'), as said below
- corner_map: int32 [8, 32, 48], P('cluster', 'sub'), may hold values from 0 to 127, as said below
- interface_tiles: int32 [8, 32, 4], P('cluster', 'sub'), may hold values from 1 to 4, as said below
- gap_terms: float32 [8, 32, 2048, 128], P('cluster', 'sub')
Outputs:
- multipliers: float32 [8, 32, 2048, 128], P('cluster', 'sub')
- residual: float32 [8, 32, 2048, 128], P('cluster', 'sub')
The draws below stay inside these ranges and needn't reach their ends.
Inputs may be any that keep to these rules, and one draw needn't show every extreme that they name: interface_tiles[c, s, k] counts the tiles that subdomain (c, s) shares with the subdomain at sub distance -2, -1, +1, +2 for k = 0..3, wrapping around 32; the count for distance +d equals that neighbour's count for distance -d; in every c some subdomain has 4 for all four. `corner_map`: the 48 entries of one subdomain are distinct. `dual_ops`: each matrix is symmetric positive definite. `coarse_inverse`: each matrix is symmetric positive definite.
All inputs are finite; a program needn't handle non-finite values.
Results may differ from the reference program's by a relative error of at most 0.009.
Values sent between devices are 32-bit elements; how exact they have to be, the bound alone decides.
No kernel may reach another device: no remote copies, remote signals or barrier semaphores. Data moves between devices by JAX's collectives and lax.ppermute only.
A program may use at most 64 MiB of HBM per device.

```python
import jax
import jax.numpy as jnp
from jax import lax

ORDER = 2048
TILE = 128
MAXT = 4
LOADS = 128
NCORN = 48
NCOARSE = 128
ITERS = 3
GROUPS = 8
CYCLE = 32


def definite_matrix(sub_key, dimension, base_diag, low_extra, ratio):
    first_key, second_key = jax.random.split(sub_key)
    spread = 0.3 * (2.0 / dimension) ** 0.5
    entries = spread * jnp.clip(jax.random.normal(first_key, (dimension, dimension), jnp.float32), -3.5, 3.5)
    symmetric = 0.5 * (entries + entries.T)
    uniform_draw = jax.random.uniform(second_key, (dimension,), jnp.float32)
    diag_extra = low_extra * ratio ** uniform_draw
    identity = jnp.eye(dimension, dtype=jnp.float32)
    return symmetric * (1.0 - identity) + identity * (base_diag + diag_extra)[:, None]


def draw_dual_ops(key, part):
    device_keys = jax.random.split(jax.random.fold_in(key, 3), GROUPS * CYCLE)
    ratio = 16.0
    matrices = lax.map(lambda sub_key: definite_matrix(sub_key, ORDER, 0.9, 0.1, ratio).astype(jnp.bfloat16), device_keys)
    return matrices.reshape(GROUPS, CYCLE, ORDER, ORDER)


def draw_coarse_inverse(key, part):
    group_keys = jax.random.split(jax.random.fold_in(key, 5), CYCLE)
    ratio = 8.0
    return lax.map(lambda sub_key: definite_matrix(sub_key, NCOARSE, 0.9, 0.1, ratio), group_keys)


def draw_corner_map(key, part):
    device_keys = jax.random.split(jax.random.fold_in(key, 7), GROUPS * CYCLE)
    chosen = jax.vmap(lambda sub_key: jax.random.permutation(sub_key, NCOARSE)[:NCORN])(device_keys)
    return chosen.reshape(GROUPS, CYCLE, NCORN).astype(jnp.int32)


def draw_interface_tiles(key, part):
    first_key = jax.random.fold_in(key, 11)
    second_key = jax.random.fold_in(key, 12)
    edge_counts = jax.random.randint(first_key, (GROUPS, CYCLE, 2), 1, MAXT + 1)
    anchor = jax.random.randint(second_key, (GROUPS, 1), 0, CYCLE)
    cycle_index = jnp.arange(CYCLE)[None, :]
    near_mask = (cycle_index == anchor) | (cycle_index == (anchor - 1) % CYCLE)
    far_mask = (cycle_index == anchor) | (cycle_index == (anchor - 2) % CYCLE)
    near_edges = jnp.where(near_mask, MAXT, edge_counts[..., 0])
    far_edges = jnp.where(far_mask, MAXT, edge_counts[..., 1])
    stacked = jnp.stack([jnp.roll(far_edges, 2, axis=1), jnp.roll(near_edges, 1, axis=1), near_edges, far_edges], axis=-1)
    return stacked.astype(jnp.int32)


def draw_gap_terms(key, part):
    first_key = jax.random.fold_in(key, 21)
    second_key = jax.random.fold_in(key, 22)
    third_key = jax.random.fold_in(key, 23)
    pattern = jax.random.normal(first_key, (GROUPS, CYCLE, ORDER, LOADS), jnp.float32)
    row_scale = 0.3 * 10.0 ** jax.random.uniform(second_key, (GROUPS, CYCLE, ORDER, 1), jnp.float32)
    column_scale = 0.3 * 10.0 ** jax.random.uniform(third_key, (1, 1, 1, LOADS), jnp.float32)
    position = (jnp.arange(GROUPS, dtype=jnp.float32)[:, None] * CYCLE + jnp.arange(CYCLE, dtype=jnp.float32)[None, :]) / max(GROUPS * CYCLE - 1, 1)
    device_scale = 0.5 * 3.0 ** position
    return pattern * row_scale * column_scale * device_scale[:, :, None, None]


def levels(rng, extent, pieces, least, high):
    def one(dim, blocks):
        draws = jax.random.uniform(jax.random.fold_in(jax.random.fold_in(rng, 6), dim), (blocks,), jnp.float32, least / len(pieces), high / len(pieces))
        return jnp.repeat(jnp.exp(draws), extent[dim] // blocks).reshape((-1,) + (1,) * (len(extent) - dim - 1))

    gain = one(*pieces[0])
    for cut in pieces[1:]:
        gain = gain * one(*cut)
    return gain


def gaussian(key, dims, scale, limit, cuts=(), kind=jnp.bfloat16):
    gain = levels(key, dims, cuts, -0.22, 0.18) if cuts else 1.0
    result = jax.random.normal(key, dims, jnp.float32) * scale * gain
    return jnp.minimum(jnp.maximum(result, -limit), limit).astype(kind)


def setup_inputs(seed: int = 0) -> dict:
    keys = jax.random.split(jax.random.key(seed), 7)
    dual_ops = draw_dual_ops(jax.random.fold_in(keys[6], 71), 0)
    corner_coupling = gaussian(keys[1], (GROUPS, CYCLE, NCORN, ORDER), 0.05, 0.3, ((0, 8), (1, 32)), jnp.float32)
    coarse_inverse = draw_coarse_inverse(jax.random.fold_in(keys[6], 71), 0)
    corner_map = draw_corner_map(jax.random.fold_in(keys[6], 71), 0)
    interface_tiles = draw_interface_tiles(jax.random.fold_in(keys[6], 71), 0)
    gap_terms = draw_gap_terms(jax.random.fold_in(keys[6], 71), 0)
    return dict(dual_ops=dual_ops, corner_coupling=corner_coupling, coarse_inverse=coarse_inverse, corner_map=corner_map, interface_tiles=interface_tiles, gap_terms=gap_terms)


def extract_run(values_in, start_row, row_count):
    run_block = lax.dynamic_slice_in_dim(values_in, start_row, MAXT * TILE, 0)
    keep_mask = jnp.arange(MAXT * TILE, dtype=jnp.int32)[:, None] < row_count
    return jnp.where(keep_mask, run_block, jnp.zeros_like(run_block))


def insert_run(run_block, start_row):
    padded = jnp.zeros((ORDER + MAXT * TILE, run_block.shape[1]), run_block.dtype)
    return lax.dynamic_update_slice_in_dim(padded, run_block, start_row, 0)[:ORDER]


def reference(dual_ops, corner_coupling, coarse_inverse, corner_map, interface_tiles, gap_terms):
    highest = lax.Precision.HIGHEST
    lengths = (interface_tiles * TILE).astype(jnp.int32)
    run_start = jnp.concatenate([jnp.zeros_like(lengths[..., :1]), jnp.cumsum(lengths, axis=-1)[..., :3].astype(jnp.int32)], axis=-1).astype(jnp.int32)
    live_rows = jnp.sum(lengths, axis=-1).astype(jnp.int32)
    live_mask = jnp.arange(ORDER, dtype=jnp.int32)[None, None, :, None] < live_rows[:, :, None, None]
    onehot = (corner_map[..., None] == jnp.arange(NCOARSE, dtype=jnp.int32)).astype(jnp.float32)

    def assemble(values_in):
        run_blocks = [jax.vmap(jax.vmap(extract_run))(values_in, run_start[..., idx], lengths[..., idx]) for idx in range(4)]
        assembled = jnp.where(live_mask, values_in, jnp.zeros_like(values_in))
        for run_index, distance in enumerate((-2, -1, 1, 2)):
            incoming = jnp.roll(run_blocks[3 - run_index], -distance, axis=1)
            assembled = assembled + jax.vmap(jax.vmap(insert_run))(incoming, run_start[..., run_index])
        return assembled

    def apply_dual(direction):
        rounded = direction.astype(jnp.bfloat16)
        local_part = lax.map(lambda operands: jnp.dot(operands[0], operands[1], preferred_element_type=jnp.float32),
                             (dual_ops.reshape(-1, ORDER, ORDER), rounded.reshape(-1, ORDER, direction.shape[-1])))
        local_part = local_part.reshape(direction.shape)
        corner_values = jnp.einsum("gsko,gsol->gskl", corner_coupling, direction, precision=highest)
        coarse_load = jnp.einsum("gskc,gskl->scl", onehot, corner_values, precision=highest)
        coarse_solution = jnp.einsum("scd,sdl->scl", coarse_inverse, coarse_load, precision=highest)
        corner_back = jnp.einsum("gskc,scl->gskl", onehot, coarse_solution, precision=highest)
        combined = local_part + jnp.einsum("gsko,gskl->gsol", corner_coupling, corner_back, precision=highest)
        return assemble(combined)

    residual = assemble(gap_terms)
    direction = residual
    multipliers = jnp.zeros_like(residual)
    norm_now = jnp.sum(residual * residual, axis=(0, 1, 2))
    for iteration in range(ITERS):
        image = apply_dual(direction)
        step_size = norm_now / jnp.sum(direction * image, axis=(0, 1, 2))
        multipliers = multipliers + step_size * direction
        residual = residual - step_size * image
        norm_next = jnp.sum(residual * residual, axis=(0, 1, 2))
        direction = residual + (norm_next / norm_now) * direction
        norm_now = norm_next
    return multipliers, residual
```

```python
import functools

import jax
import jax.numpy as jnp
from jax import lax
from jax.experimental import pallas as pl
from jax.experimental.pallas import tpu as pltpu
from jax.sharding import PartitionSpec as P

TILE = 128
MAXT = 4
RUNS = 4
NCOARSE = 128
EXTRA = 8
SCALE = 1.0 / 32.0
DISTANCES = (-2, -1, 1, 2)

VMEM = pl.BlockSpec(memory_space=pltpu.VMEM)
SMEM = pl.BlockSpec(memory_space=pltpu.SMEM)
F32 = jnp.float32
BF16 = jnp.bfloat16


def params(mebibytes=4):
    return pltpu.CompilerParams(vmem_limit_bytes=mebibytes * 1024 * 1024)


def halves(x):
    high = x.astype(BF16)
    low = (x - high.astype(F32)).astype(BF16)
    return high, low


def dot(a, b):
    return jnp.dot(a, b, preferred_element_type=F32)


def run_starts(tiles):
    starts = [0]
    for k in range(RUNS):
        starts.append(starts[-1] + tiles[k])
    return starts


def tile_rows(tile):
    return pl.ds(pl.multiple_of(tile * TILE, TILE), TILE)


def take_runs(tiles, source, outs):
    starts = run_starts(tiles)
    for k in range(RUNS):
        for j in range(MAXT):
            outs[k][j * TILE:(j + 1) * TILE, :] = source[tile_rows(starts[k] + j), :]


def gap_kernel(tiles, gap, *outs):
    take_runs(tiles, gap, outs)


def each_tile(tiles, rows, live, padding):
    starts = run_starts(tiles)
    for k in range(RUNS):
        for j in range(MAXT):
            @pl.when(j < tiles[k])
            def _(k=k, j=j):
                live(tile_rows(starts[k] + j), k, slice(j * TILE, (j + 1) * TILE))
    for t in range(RUNS, rows // TILE):
        @pl.when(t >= starts[RUNS])
        def _(t=t):
            padding(slice(t * TILE, (t + 1) * TILE))


def column_sum(x):
    return jnp.sum(x, axis=0, keepdims=True)


def assemble_kernel(step, tiles, own, in0, in1, in2, in3, coupling, extra, *rest):
    if step == 0:
        field, split, payload, moments = rest
        previous = None
    else:
        previous, old_moments, field, split, payload, moments = rest
    incoming = (in0, in1, in2, in3)
    rows = own.shape[0]

    def live(where, k, block):
        x = own[where, :] + incoming[k][block, :]
        field[where, :] = x
        high, low = halves(x)
        split[where, 0:TILE] = high
        split[where, TILE:2 * TILE] = low

    def padding(where):
        field[where, :] = jnp.zeros((TILE, field.shape[1]), F32)
        split[where, :] = jnp.zeros((TILE, split.shape[1]), BF16)

    each_tile(tiles, rows, live, padding)
    values = field[...]
    if step == 0:
        moments[...] = jnp.zeros(moments.shape, F32)
        moments[0:1, :] = column_sum(values * values)
    else:
        moments[...] = old_moments[...]
        moments[2 * step - 1:2 * step, :] = column_sum(values * previous[...])
        moments[2 * step:2 * step + 1, :] = column_sum(values * values)
    product = dot(coupling[...], split[...])
    corners = coupling.shape[0] // 2
    values = (product[:corners, :TILE] + product[corners:, :TILE]) + (
        product[:corners, TILE:] + product[corners:, TILE:]
    )
    for peer in range(payload.shape[0]):
        payload[peer, 0:corners, :] = values
        if step == 0:
            payload[peer, corners:, :] = extra[...]


def assemble(step, tiles, own, incoming, coupling, extra, previous, old_moments, peers):
    rows, loads = own.shape
    corners = coupling.shape[0] // 2
    depth = corners + (EXTRA if step == 0 else 0)
    more = () if step == 0 else (previous, old_moments)
    return pl.pallas_call(
        functools.partial(assemble_kernel, step),
        out_shape=(
            jax.ShapeDtypeStruct((rows, loads), F32),
            jax.ShapeDtypeStruct((rows, 2 * loads), BF16),
            jax.ShapeDtypeStruct((peers, depth, loads), F32),
            jax.ShapeDtypeStruct((EXTRA, loads), F32),
        ),
        in_specs=[SMEM] + [VMEM] * (7 + len(more)),
        out_specs=(VMEM,) * 4,
        compiler_params=params(),
        name=f"assemble{step}",
    )(tiles, own, *incoming, coupling, extra, *more)


def local_kernel(block, with_sum, operator, split, *rest):
    if with_sum:
        field, moments, out, sums = rest
    else:
        (out,) = rest
    loads = out.shape[1]

    def body(i, total):
        where = pl.ds(pl.multiple_of(i * block, block), block)
        product = dot(operator[where, :], split[...])
        value = product[:, :loads] + product[:, loads:]
        out[where, :] = value
        return total + column_sum(value * field[where, :]) if with_sum else total

    total = lax.fori_loop(0, out.shape[0] // block, body, jnp.zeros((1, loads), F32))
    if with_sum:
        sums[...] = moments[...]
        sums[5:6, :] = total


def local_product(operator, split, field=None, moments=None):
    rows = operator.shape[0]
    loads = split.shape[1] // 2
    cost = pl.CostEstimate(
        flops=4 * rows * rows * loads, bytes_accessed=2 * rows * rows + 8 * rows * loads, transcendentals=0
    )
    with_sum = field is not None
    out_shape = [jax.ShapeDtypeStruct((rows, loads), F32)]
    more = ()
    if with_sum:
        out_shape.append(jax.ShapeDtypeStruct((EXTRA, loads), F32))
        more = (field, moments)
    result = pl.pallas_call(
        functools.partial(local_kernel, 256, with_sum),
        out_shape=tuple(out_shape), in_specs=[VMEM] * (2 + len(more)), out_specs=(VMEM,) * len(out_shape),
        compiler_params=params(), cost_estimate=cost, name="local_sum" if with_sum else "local_product",
    )(operator, split, *more)
    return result if with_sum else result[0]


def stacked(x):
    high, low = halves(x)
    row = jnp.concatenate([high, low], axis=1)
    return jnp.concatenate([row, row], axis=0)


def coarse_kernel(last, corners, tiles, gathered, maps, own_map, inverse, coupling_t, local_part, *rest):
    if last:
        gathered_moments, combined, out0, out1, out2, out3, sums = rest
    else:
        combined, out0, out1, out2, out3 = rest
    peers = gathered.shape[0]
    loads = gathered.shape[2]
    index = lax.broadcasted_iota(jnp.int32, (NCOARSE, corners), 0).astype(F32)
    load = jnp.zeros((NCOARSE, 2 * loads), F32)
    for peer in range(peers):
        choose = (index == maps[peer, corners:corners + 1, :corners]).astype(BF16)
        high, low = halves(gathered[peer, 0:corners, :])
        load = load + dot(choose, jnp.concatenate([high, low], axis=1))
    load = load[:, :loads] + load[:, loads:]
    high, low = halves(inverse[...])
    solved = dot(jnp.concatenate([high, low], axis=1), stacked(load))
    solved = solved[:, :loads] + solved[:, loads:]
    choose = (index == own_map[0:1, :corners]).astype(BF16)
    high, low = halves(solved)
    back = lax.dot_general(
        choose, jnp.concatenate([high, low], axis=1), (((0,), (0,)), ((), ())), preferred_element_type=F32
    )
    back = back[:, :loads] + back[:, loads:]
    product = dot(coupling_t[...], stacked(back))
    combined[...] = (local_part[...] + (product[:, :loads] + product[:, loads:])) * SCALE
    take_runs(tiles, combined, (out0, out1, out2, out3))
    if last:
        total = gathered_moments[0]
        for peer in range(1, peers):
            total = total + gathered_moments[peer]
        row = lax.broadcasted_iota(jnp.int32, total.shape, 0)
        quad = column_sum(load * solved)
        total = jnp.where(row == 5, (total + quad) * (2.0 * SCALE), total)
        for peer in range(sums.shape[0]):
            sums[peer] = total


def coarse(last, corners, tiles, gathered, maps, own_map, inverse, coupling_t, local_part, gathered_moments, sub_peers):
    rows, loads = local_part.shape
    out_shape = [jax.ShapeDtypeStruct((rows, loads), F32)]
    out_shape += [jax.ShapeDtypeStruct((MAXT * TILE, loads), F32)] * RUNS
    more = ()
    if last:
        out_shape.append(jax.ShapeDtypeStruct((sub_peers, EXTRA, loads), F32))
        more = (gathered_moments,)
    return pl.pallas_call(
        functools.partial(coarse_kernel, last, corners),
        out_shape=tuple(out_shape),
        in_specs=[SMEM] + [VMEM] * (6 + len(more)),
        out_specs=(VMEM,) * len(out_shape),
        compiler_params=params(),
        name="coarse_last" if last else "coarse",
    )(tiles, gathered, maps, own_map, inverse, coupling_t, local_part, *more)


def inner(m, p, q, lift):
    total = None
    for i in range(len(p)):
        for j in range(len(q)):
            term = p[i] * q[j] * m[i + j + lift]
            total = term if total is None else total + term
    return total


def coefficients(m):
    one = jnp.ones_like(m[0])
    res, dire, mult = [one], [one], []
    norm = m[0]
    for step in range(3):
        size = norm / inner(m, dire, dire, 1)
        mult = [
            (mult[i] if i < len(mult) else 0.0) + size * dire[i] for i in range(len(dire))
        ]
        grown = []
        for i in range(len(dire) + 1):
            value = res[i] if i < len(res) else jnp.zeros_like(one)
            grown.append(value - size * dire[i - 1] if i > 0 else value)
        res = grown
        if step < 2:
            fresh = inner(m, res, res, 0)
            ratio = fresh / norm
            dire = [res[i] + ratio * dire[i] if i < len(dire) else res[i] for i in range(len(res))]
            norm = fresh
    return mult, res


def final_kernel(tiles, own, in0, in1, in2, in3, v0, v1, v2, gathered, out_mult, out_res):
    incoming = (in0, in1, in2, in3)
    total = gathered[0]
    for peer in range(1, gathered.shape[0]):
        total = total + gathered[peer]
    mult, res = coefficients([total[i:i + 1, :] for i in range(6)])
    mult = [c * SCALE for c in mult]

    def live(where, k, block):
        a, b, c = v0[where, :], v1[where, :], v2[where, :]
        d = own[where, :] + incoming[k][block, :]
        out_mult[where, :] = a * mult[0] + b * mult[1] + c * mult[2]
        out_res[where, :] = a * res[0] + b * res[1] + c * res[2] + d * res[3]

    def padding(where):
        zero = jnp.zeros((TILE, own.shape[1]), F32)
        out_mult[where, :] = zero
        out_res[where, :] = zero

    each_tile(tiles, own.shape[0], live, padding)


def exchange(outs):
    size = lax.axis_size("sub")
    incoming = []
    for k, distance in enumerate(DISTANCES):
        route = [((i + distance) % size, i) for i in range(size)]
        incoming.append(lax.ppermute(outs[RUNS - 1 - k], "sub", route))
    return incoming


def swap(blocks, axis):
    return lax.all_to_all(blocks, axis, 0, 0)


def local(dual_ops, corner_coupling, coarse_inverse, corner_map, interface_tiles, gap_terms):
    operator = dual_ops[0, 0]
    inverse = coarse_inverse[0]
    tiles = interface_tiles[0, 0]
    gap = gap_terms[0, 0]
    rows, loads = gap.shape
    corners = corner_map.shape[-1]
    peers = lax.axis_size("cluster")
    sub_peers = lax.axis_size("sub")

    run = jax.ShapeDtypeStruct((MAXT * TILE, loads), F32)
    outs = pl.pallas_call(
        gap_kernel, out_shape=(run,) * RUNS, in_specs=[SMEM, VMEM], out_specs=(VMEM,) * RUNS,
        compiler_params=params(), name="gap_runs",
    )(tiles, gap)
    incoming = exchange(outs)

    high = lax.reduce_precision(corner_coupling[0, 0], 8, 7)
    coupling = jnp.concatenate([high, corner_coupling[0, 0] - high], axis=0).astype(BF16)
    coupling_t = coupling.T
    own_map = jnp.pad(corner_map[0, 0].astype(F32)[None, :], ((0, EXTRA - 1), (0, loads - corners)))

    own = gap
    fields, moments, maps = [], None, None
    for step in range(3):
        previous = fields[-1] if fields else None
        field, split, payload, moments = assemble(
            step, tiles, own, incoming, coupling, own_map, previous, moments, peers
        )
        fields.append(field)
        last = step == 2
        gathered_moments = None
        if last:
            local_part, sums = local_product(operator, split, field, moments)
            payload = jnp.concatenate([payload, jnp.broadcast_to(sums[None], (peers, EXTRA, loads))], axis=1)
            gathered = swap(payload, "cluster")
            gathered_moments = gathered[:, corners:]
        else:
            gathered = swap(payload, "cluster")
            local_part = local_product(operator, split)
        if step == 0:
            maps = gathered
        result = coarse(
            last, corners, tiles, gathered, maps, own_map, inverse, coupling_t, local_part,
            gathered_moments, sub_peers,
        )
        own, outs = result[0], result[1:1 + RUNS]
        incoming = exchange(outs)
    totals = swap(result[1 + RUNS], "sub")
    whole = jax.ShapeDtypeStruct((rows, loads), F32)
    multipliers, residual = pl.pallas_call(
        final_kernel, out_shape=(whole, whole), in_specs=[SMEM] + [VMEM] * 9, out_specs=(VMEM, VMEM),
        compiler_params=params(), name="final",
    )(tiles, own, *incoming, *fields, totals)
    return (multipliers[None, None], residual[None, None])


def solution(mesh):
    in_specs = (
        P("cluster", "sub", None, None),
        P("cluster", "sub", None, None),
        P("sub", None, None),
        P("cluster", "sub", None),
        P("cluster", "sub", None),
        P("cluster", "sub", None, None),
    )
    out_specs = (P("cluster", "sub", None, None), P("cluster", "sub", None, None))
    return jax.shard_map(local, mesh=mesh, in_specs=in_specs, out_specs=out_specs, check_vma=False)
```

```python
import functools

import jax
import jax.numpy as jnp
from jax import lax
from jax.experimental import pallas as pl
from jax.experimental.pallas import tpu as pltpu
from jax.sharding import PartitionSpec as P

TILE = 128
MAXT = 4
RUNS = 4
NCOARSE = 128
EXTRA = 8
SCALE = 1.0 / 32.0
DISTANCES = (-2, -1, 1, 2)

VMEM = pl.BlockSpec(memory_space=pltpu.VMEM)
SMEM = pl.BlockSpec(memory_space=pltpu.SMEM)
HBM = pl.BlockSpec(memory_space=pltpu.HBM)
F32 = jnp.float32
BF16 = jnp.bfloat16
CHUNK = 256
BLOCK = 512
AHEAD = 2


def in_hbm(x):
    return pltpu.with_memory_space_constraint(x, pltpu.HBM)


def params(mebibytes):
    return pltpu.CompilerParams(vmem_limit_bytes=mebibytes * 1024 * 1024)


def halves(x):
    high = x.astype(BF16)
    low = (x - high.astype(F32)).astype(BF16)
    return high, low


def dot(a, b):
    return jnp.dot(a, b, preferred_element_type=F32)


def column_sum(x):
    return jnp.sum(x, axis=0, keepdims=True)


def run_starts(tiles):
    starts = [0]
    for k in range(RUNS):
        starts.append(starts[-1] + tiles[k])
    return starts


def tile_rows(tile, count=1):
    return pl.ds(pl.multiple_of(tile * TILE, TILE), count * TILE)


def each_tile(tiles, rows, live, padding):
    starts = run_starts(tiles)
    for k in range(RUNS):
        for j in range(MAXT):
            @pl.when(j < tiles[k])
            def _(k=k, j=j):
                live(tile_rows(starts[k] + j), k, slice(j * TILE, (j + 1) * TILE))
    if padding is None:
        return
    for t in range(RUNS, rows // TILE):
        @pl.when(t >= starts[RUNS])
        def _(t=t):
            padding(slice(t * TILE, (t + 1) * TILE))


class Pieces:
    def __init__(self, source, target, sems, first=0, size=CHUNK):
        self.copies = []
        for i in range(source.shape[0] // size):
            where = slice(i * size, (i + 1) * size)
            self.copies.append(
                pltpu.make_async_copy(source.at[where, :], target.at[where, :], sems.at[first + i])
            )

    def start(self):
        for copy in self.copies:
            copy.start()

    def wait(self):
        for copy in self.copies:
            copy.wait()


def gap_kernel(tiles_hbm, gap, o0, o1, o2, o3, tiles, sem_tiles, sems):
    fetch = pltpu.make_async_copy(tiles_hbm, tiles, sem_tiles)
    fetch.start()
    fetch.wait()
    starts = run_starts(tiles)
    copies = []
    for k, out in enumerate((o0, o1, o2, o3)):
        for j in range(MAXT):
            copies.append(
                pltpu.make_async_copy(
                    gap.at[tile_rows(starts[k] + j), :], out.at[j * TILE:(j + 1) * TILE, :],
                    sems.at[k * MAXT + j],
                )
            )
    for copy in copies:
        copy.start()
    for copy in copies:
        copy.wait()


def gap_runs(tiles, gap):
    run = jax.ShapeDtypeStruct((MAXT * TILE, gap.shape[1]), F32)
    return pl.pallas_call(
        gap_kernel, out_shape=(run,) * RUNS, in_specs=[HBM, HBM], out_specs=(VMEM,) * RUNS,
        scratch_shapes=[
            pltpu.SMEM((RUNS,), jnp.int32), pltpu.SemaphoreType.DMA(()), pltpu.SemaphoreType.DMA((RUNS * MAXT,))
        ], compiler_params=params(2), name="gap_runs",
    )(in_hbm(tiles), gap)


def prepare_kernel(tiles, coupling, corner_map, pair, turned, own_map, tiles_out):
    for k in range(RUNS):
        tiles_out[k] = tiles[k]
    corners, rows = coupling.shape
    high, low = halves(coupling[...])
    pair[0:corners, :] = high
    pair[corners:2 * corners, :] = low
    depth = turned.shape[1]
    for t in range(rows // TILE):
        block = coupling[:, t * TILE:(t + 1) * TILE]
        top = block.astype(BF16).astype(F32)
        rest = jnp.zeros((depth - 2 * corners, TILE), F32)
        stack = jnp.concatenate([top, block - top, rest], axis=0)
        turned[t * TILE:(t + 1) * TILE, :] = stack.T.astype(BF16)
    own_map[...] = jnp.zeros(own_map.shape, F32)
    own_map[0:1, 0:corners] = corner_map[...].astype(F32)


def prepare(tiles, coupling, corner_map, loads):
    corners, rows = coupling.shape
    return pl.pallas_call(
        prepare_kernel,
        out_shape=(
            jax.ShapeDtypeStruct((2 * corners, rows), BF16),
            jax.ShapeDtypeStruct((rows, TILE), BF16),
            jax.ShapeDtypeStruct((EXTRA, loads), F32),
            jax.ShapeDtypeStruct((RUNS,), jnp.int32),
        ),
        in_specs=[SMEM, VMEM, VMEM],
        out_specs=(VMEM, VMEM, VMEM, SMEM),
        compiler_params=params(8),
        cost_estimate=pl.CostEstimate(flops=10**6, bytes_accessed=8 * 10**6, transcendentals=0),
        name="prepare",
    )(tiles, coupling, corner_map)


def build_field(tiles, outs, incoming, field, split):
    def live(where, k, block):
        x = outs[k][block, :] + incoming[k][block, :]
        field[where, :] = x
        high, low = halves(x)
        split[where, 0:TILE] = high
        split[where, TILE:2 * TILE] = low

    def padding(where):
        field[where, :] = jnp.zeros((TILE, field.shape[1]), F32)
        split[where, :] = jnp.zeros((TILE, split.shape[1]), BF16)

    each_tile(tiles, field.shape[0], live, padding)


def corner_values(pair, split):
    product = dot(pair[...], split[...])
    corners = pair.shape[0] // 2
    return (product[:corners, :TILE] + product[corners:, :TILE]) + (
        product[:corners, TILE:] + product[corners:, TILE:]
    )


def spread(values, payload, sems):
    copies = [
        pltpu.make_async_copy(values, payload.at[peer], sems.at[peer]) for peer in range(payload.shape[0])
    ]
    for copy in copies:
        copy.start()
    return copies


def assemble_kernel(first, tiles, o0, o1, o2, o3, i0, i1, i2, i3, pair, *rest):
    if first:
        extra, field_hbm, payload, field, split, values, sem_out, sems = rest
    else:
        field_hbm, payload, field, split, values, sem_out, sems = rest
    build_field(tiles, (o0, o1, o2, o3), (i0, i1, i2, i3), field, split)
    keep = Pieces(field, field_hbm, sem_out, size=2 * CHUNK)
    keep.start()
    corners = pair.shape[0] // 2
    values[0:corners, :] = corner_values(pair, split)
    if first:
        values[corners:, :] = extra[...]
    copies = spread(values, payload, sems)
    for copy in copies:
        copy.wait()
    keep.wait()


def assemble(first, tiles, outs, incoming, pair, extra, rows, peers):
    loads = outs[0].shape[1]
    corners = pair.shape[0] // 2
    depth = corners + (EXTRA if first else 0)
    more = (extra,) if first else ()
    return pl.pallas_call(
        functools.partial(assemble_kernel, first),
        out_shape=(pltpu.HBM((rows, loads), F32), pltpu.HBM((peers, depth, loads), F32)),
        in_specs=[SMEM] + [VMEM] * (2 * RUNS + 1 + len(more)),
        out_specs=(HBM, HBM),
        scratch_shapes=[
            pltpu.VMEM((rows, loads), F32),
            pltpu.VMEM((rows, 2 * loads), BF16),
            pltpu.VMEM((depth, loads), F32),
            pltpu.SemaphoreType.DMA((rows // CHUNK,)),
            pltpu.SemaphoreType.DMA((peers,)),
        ],
        compiler_params=params(6),
        name="assemble_first" if first else "assemble",
    )(tiles, *outs, *incoming, pair, *more)


def operator_copy(operator_hbm, operator, sems, i):
    where = pl.ds(pl.multiple_of(i * CHUNK, CHUNK), CHUNK)
    return pltpu.make_async_copy(operator_hbm.at[where, :], operator.at[where, :], sems.at[i])


def local_kernel(step, operator_hbm, field_hbm, *rest):
    if step == 0:
        out, moments, operator, field, split, sem_field, sems = rest
    else:
        previous_hbm, old, out, moments, operator, field, split, previous, sem_field, sems, sem_previous = rest
    fetch = pltpu.make_async_copy(field_hbm, field, sem_field)
    fetch.start()
    rows, loads = out.shape
    count = rows // BLOCK

    def piece(i):
        where = pl.ds(pl.multiple_of(i * BLOCK, BLOCK), BLOCK)
        return pltpu.make_async_copy(operator_hbm.at[where, :], operator.at[where, :], sems.at[i])

    for i in range(AHEAD):
        piece(i).start()
    if step > 0:
        fetch_previous = pltpu.make_async_copy(previous_hbm, previous, sem_previous)
    fetch.wait()
    square = cross = jnp.zeros((1, loads), F32)
    for i in range(rows // CHUNK):
        where = slice(i * CHUNK, (i + 1) * CHUNK)
        x = field[where, :]
        high, low = halves(x)
        split[where, 0:TILE] = high
        split[where, TILE:2 * TILE] = low
        square = square + column_sum(x * x)
    def body(i, carry):
        piece(i).wait()

        @pl.when(i + AHEAD < count)
        def _():
            piece(i + AHEAD).start()

        where = pl.ds(pl.multiple_of(i * BLOCK, BLOCK), BLOCK)
        product = dot(operator[where, :], split[...])
        out[where, :] = product[:, :loads] + product[:, loads:]
        return carry

    lax.fori_loop(0, count, body, 0)
    if step > 0:
        fetch_previous.start()
        fetch_previous.wait()
        cross = column_sum(field[...] * previous[...])
    if step == 0:
        moments[...] = jnp.zeros(moments.shape, F32)
        moments[0:1, :] = square
    else:
        moments[...] = old[...]
        moments[1:2, :] = cross
        moments[2:3, :] = square


def product_cost(rows, loads):
    return pl.CostEstimate(
        flops=4 * rows * rows * loads, bytes_accessed=2 * rows * rows + 8 * rows * loads, transcendentals=0
    )


def local_product(step, operator, field, previous=None, moments=None):
    rows, loads = field.shape
    pieces, single = pltpu.SemaphoreType.DMA((rows // CHUNK,)), pltpu.SemaphoreType.DMA(())
    more, more_specs, more_scratch, more_sems = (), [], [], []
    if step > 0:
        more, more_specs = (in_hbm(previous), moments), [HBM, VMEM]
        more_scratch, more_sems = [pltpu.VMEM((rows, loads), F32)], [single]
    return pl.pallas_call(
        functools.partial(local_kernel, step),
        out_shape=(jax.ShapeDtypeStruct((rows, loads), F32), jax.ShapeDtypeStruct((EXTRA, loads), F32)),
        in_specs=[HBM, HBM] + more_specs,
        out_specs=(VMEM, VMEM),
        scratch_shapes=[
            pltpu.VMEM(operator.shape, BF16),
            pltpu.VMEM((rows, loads), F32),
            pltpu.VMEM((rows, 2 * loads), BF16),
            *more_scratch,
            single,
            pieces,
            *more_sems,
        ],
        compiler_params=params(16),
        cost_estimate=product_cost(rows, loads),
        name=f"local_product{step}",
    )(operator, in_hbm(field), *more)


def load_kernel(operator_hbm, token, operator, sem):
    del token
    fetch = pltpu.make_async_copy(operator_hbm, operator, sem)
    fetch.start()
    fetch.wait()


def load_operator(operator, token):
    return pl.pallas_call(
        load_kernel, out_shape=pltpu.VMEM(operator.shape, BF16), in_specs=[HBM, HBM], out_specs=VMEM,
        scratch_shapes=[pltpu.SemaphoreType.DMA(())],
        compiler_params=params(2), cost_estimate=product_cost(operator.shape[0], TILE), name="load_operator",
    )(operator, token)


def joint_kernel(
    tiles, o0, o1, o2, o3, i0, i1, i2, i3, pair, operator, previous_hbm, old,
    field, payload, out, split, previous, sem_previous,
):
    fetch_previous = Pieces(previous_hbm, previous, sem_previous)
    fetch_previous.start()
    build_field(tiles, (o0, o1, o2, o3), (i0, i1, i2, i3), field, split)
    corners = pair.shape[0] // 2
    loads = out.shape[1]
    values = corner_values(pair, split)
    for peer in range(payload.shape[0]):
        payload[peer, 0:corners, :] = values
    fetch_previous.wait()
    zero = jnp.zeros((1, loads), F32)

    def body(i, totals):
        where = pl.ds(pl.multiple_of(i * BLOCK, BLOCK), BLOCK)
        product = dot(operator[where, :], split[...])
        value = product[:, :loads] + product[:, loads:]
        out[where, :] = value
        x = field[where, :]
        return (
            totals[0] + column_sum(x * previous[where, :]),
            totals[1] + column_sum(x * x),
            totals[2] + column_sum(x * value),
        )

    cross, square, local_sum = lax.fori_loop(0, out.shape[0] // BLOCK, body, (zero, zero, zero))
    row = lax.broadcasted_iota(jnp.int32, old.shape, 0)
    sums = old[...]
    for index, value in ((3, cross), (4, square), (5, local_sum)):
        sums = jnp.where(row == index, value, sums)
    for peer in range(payload.shape[0]):
        payload[peer, corners:, :] = sums


def joint(tiles, outs, incoming, pair, operator, previous, moments, peers):
    rows, loads = previous.shape
    depth = pair.shape[0] // 2 + EXTRA
    return pl.pallas_call(
        joint_kernel,
        out_shape=(
            jax.ShapeDtypeStruct((rows, loads), F32),
            jax.ShapeDtypeStruct((peers, depth, loads), F32),
            jax.ShapeDtypeStruct((rows, loads), F32),
        ),
        in_specs=[SMEM] + [VMEM] * (2 * RUNS) + [VMEM, VMEM, HBM, VMEM],
        out_specs=(VMEM, VMEM, VMEM),
        scratch_shapes=[
            pltpu.VMEM((rows, 2 * loads), BF16),
            pltpu.VMEM((rows, loads), F32),
            pltpu.SemaphoreType.DMA((rows // CHUNK,)),
        ],
        compiler_params=params(8),
        cost_estimate=product_cost(rows, loads),
        name="joint",
    )(tiles, *outs, *incoming, pair, operator, previous, moments)


def stacked(x):
    high, low = halves(x)
    row = jnp.concatenate([high, low], axis=1)
    return jnp.concatenate([row, row], axis=0)


def coarse_solve(gathered, maps, own_map, inverse, corners):
    loads = gathered.shape[2]
    index = lax.broadcasted_iota(jnp.int32, (NCOARSE, corners), 0).astype(F32)
    load = jnp.zeros((NCOARSE, 2 * loads), F32)
    for peer in range(gathered.shape[0]):
        choose = (index == maps[peer, 0:1, :corners]).astype(BF16)
        high, low = halves(gathered[peer, 0:corners, :])
        load = load + dot(choose, jnp.concatenate([high, low], axis=1))
    load = load[:, :loads] + load[:, loads:]
    high, low = halves(inverse[...])
    solved = dot(jnp.concatenate([high, low], axis=1), stacked(load))
    solved = solved[:, :loads] + solved[:, loads:]
    choose = (index == own_map[0:1, :corners]).astype(BF16)
    high, low = halves(solved)
    back = lax.dot_general(
        choose, jnp.concatenate([high, low], axis=1), (((0,), (0,)), ((), ())), preferred_element_type=F32
    )
    return load, solved, back[:, :loads] + back[:, loads:]


def spread_back(tiles, back, local_part, turned, product, outs):
    corners, loads = back.shape
    rest = jnp.zeros((turned.shape[1] - 2 * corners, 2 * loads), BF16)
    wide = dot(turned[...], jnp.concatenate([stacked(back), rest], axis=0))
    product[...] = wide[:, :loads] + wide[:, loads:]

    def live(where, k, block):
        outs[k][block, :] = (local_part[where, :] + product[where, :]) * SCALE

    each_tile(tiles, product.shape[0], live, None)


def coarse_kernel(step, corners, tiles, gathered, inverse, own_map, local_part, turned, *rest):
    if step == 0:
        o0, o1, o2, o3, maps, product = rest
        for peer in range(gathered.shape[0]):
            maps[peer] = gathered[peer, corners:corners + EXTRA, :]
    else:
        maps, o0, o1, o2, o3, product = rest
    back = coarse_solve(gathered, maps, own_map, inverse, corners)[2]
    spread_back(tiles, back, local_part, turned, product, (o0, o1, o2, o3))


def coarse(step, corners, tiles, gathered, own_map, inverse, local_part, turned, maps):
    rows, loads = local_part.shape
    peers = gathered.shape[0]
    out_shape = [jax.ShapeDtypeStruct((MAXT * TILE, loads), F32)] * RUNS
    more = () if step == 0 else (maps,)
    if step == 0:
        out_shape.append(jax.ShapeDtypeStruct((peers, EXTRA, loads), F32))
    return pl.pallas_call(
        functools.partial(coarse_kernel, step, corners),
        out_shape=tuple(out_shape),
        in_specs=[SMEM] + [VMEM] * (5 + len(more)),
        out_specs=(VMEM,) * len(out_shape),
        scratch_shapes=[pltpu.VMEM((rows, loads), F32)],
        compiler_params=params(6),
        name=f"coarse{step}",
    )(tiles, gathered, inverse, own_map, local_part, turned, *more)


def last_solve_kernel(corners, gathered, inverse, own_map, maps, back, sums_hbm, sums, sems):
    load, solved, value = coarse_solve(gathered, maps, own_map, inverse, corners)
    total = gathered[0, corners:corners + EXTRA, :]
    for peer in range(1, gathered.shape[0]):
        total = total + gathered[peer, corners:corners + EXTRA, :]
    row = lax.broadcasted_iota(jnp.int32, total.shape, 0)
    quad = column_sum(load * solved)
    total = jnp.where(row == 5, (total + quad) * (2.0 * SCALE), total)
    for peer in range(sums.shape[0]):
        sums[peer] = total
    keep = pltpu.make_async_copy(sums, sums_hbm, sems)
    keep.start()
    back[...] = value
    keep.wait()


def last_solve(corners, gathered, own_map, inverse, maps, sub_peers):
    loads = gathered.shape[2]
    return pl.pallas_call(
        functools.partial(last_solve_kernel, corners),
        out_shape=(jax.ShapeDtypeStruct((corners, loads), F32), pltpu.HBM((sub_peers, EXTRA, loads), F32)),
        in_specs=[VMEM] * 4, out_specs=(VMEM, HBM),
        scratch_shapes=[pltpu.VMEM((sub_peers, EXTRA, loads), F32), pltpu.SemaphoreType.DMA(())],
        compiler_params=params(4), name="last_solve",
    )(gathered, inverse, own_map, maps)


def last_spread_kernel(tiles, back, local_part, turned, o0, o1, o2, o3, product):
    spread_back(tiles, back[...], local_part, turned, product, (o0, o1, o2, o3))


def last_spread(tiles, back, local_part, turned):
    rows, loads = local_part.shape
    return pl.pallas_call(
        last_spread_kernel,
        out_shape=(jax.ShapeDtypeStruct((MAXT * TILE, loads), F32),) * RUNS,
        in_specs=[SMEM] + [VMEM] * 3, out_specs=(VMEM,) * RUNS,
        scratch_shapes=[pltpu.VMEM((rows, loads), F32)],
        compiler_params=params(6), cost_estimate=product_cost(rows // 2, loads), name="last_spread",
    )(tiles, back, local_part, turned)


def inner(m, p, q, lift):
    total = None
    for i in range(len(p)):
        for j in range(len(q)):
            term = p[i] * q[j] * m[i + j + lift]
            total = term if total is None else total + term
    return total


def coefficients(m):
    one = jnp.ones_like(m[0])
    res, dire, mult = [one], [one], []
    norm = m[0]
    for step in range(3):
        size = norm / inner(m, dire, dire, 1)
        mult = [
            (mult[i] if i < len(mult) else 0.0) + size * dire[i] for i in range(len(dire))
        ]
        grown = []
        for i in range(len(dire) + 1):
            value = res[i] if i < len(res) else jnp.zeros_like(one)
            grown.append(value - size * dire[i - 1] if i > 0 else value)
        res = grown
        if step < 2:
            fresh = inner(m, res, res, 0)
            ratio = fresh / norm
            dire = [res[i] + ratio * dire[i] if i < len(dire) else res[i] for i in range(len(res))]
            norm = fresh
    return mult, res


def final_kernel(
    tiles, o0, o1, o2, o3, i0, i1, i2, i3, v0, v1, v2, gathered, out_mult, out_res
):
    outs, incoming = (o0, o1, o2, o3), (i0, i1, i2, i3)
    total = gathered[0]
    for peer in range(1, gathered.shape[0]):
        total = total + gathered[peer]
    mult, res = coefficients([total[i:i + 1, :] for i in range(6)])
    mult = [c * SCALE for c in mult]

    def live(where, k, block):
        a, b, c = v0[where, :], v1[where, :], v2[where, :]
        d = outs[k][block, :] + incoming[k][block, :]
        out_mult[where, :] = a * mult[0] + b * mult[1] + c * mult[2]
        out_res[where, :] = a * res[0] + b * res[1] + c * res[2] + d * res[3]

    def padding(where):
        zero = jnp.zeros((TILE, out_mult.shape[1]), F32)
        out_mult[where, :] = zero
        out_res[where, :] = zero

    each_tile(tiles, out_mult.shape[0], live, padding)


def final(tiles, outs, incoming, fields, totals):
    whole = jax.ShapeDtypeStruct(fields[0].shape, F32)
    return pl.pallas_call(
        final_kernel, out_shape=(whole, whole),
        in_specs=[SMEM] + [VMEM] * (2 * RUNS + 4),
        out_specs=(VMEM, VMEM),
        compiler_params=params(4), name="final",
    )(tiles, *outs, *incoming, *fields, totals)


def exchange(outs):
    size = lax.axis_size("sub")
    incoming = []
    for k, distance in enumerate(DISTANCES):
        route = [((i + distance) % size, i) for i in range(size)]
        incoming.append(lax.ppermute(outs[RUNS - 1 - k], "sub", route))
    return incoming


def swap(blocks, axis):
    return lax.all_to_all(blocks, axis, 0, 0)


def local(dual_ops, corner_coupling, coarse_inverse, corner_map, interface_tiles, gap_terms):
    operator = in_hbm(dual_ops[0, 0])
    inverse = coarse_inverse[0]
    tiles = interface_tiles[0, 0]
    gap = in_hbm(gap_terms[0, 0])
    rows, loads = gap.shape
    corners = corner_map.shape[-1]
    peers = lax.axis_size("cluster")
    sub_peers = lax.axis_size("sub")

    outs = gap_runs(tiles, gap)
    incoming = exchange(outs)
    pair, turned, own_map, tiles = prepare(tiles, corner_coupling[0, 0], corner_map[0], loads)

    fields, moments, maps = [], None, None
    for step in range(3):
        if step < 2:
            field, payload = assemble(step == 0, tiles, outs, incoming, pair, own_map, rows, peers)
            gathered = swap(payload, "cluster")
            previous = fields[-1] if fields else None
            local_part, moments = local_product(step, operator, field, previous, moments)
        else:
            field, payload, local_part = joint(
                tiles, outs, incoming, pair, load_operator(operator, outs[0]), in_hbm(fields[-1]), moments, peers
            )
            gathered = swap(payload, "cluster")
        fields.append(field)
        if step < 2:
            outs = coarse(step, corners, tiles, gathered, own_map, inverse, local_part, turned, maps)
            if step == 0:
                outs, maps = outs[:RUNS], outs[RUNS]
        else:
            back, sums = last_solve(corners, gathered, own_map, inverse, maps, sub_peers)
            totals = swap(sums, "sub")
            outs = last_spread(tiles, back, local_part, turned)
        incoming = exchange(outs)
    multipliers, residual = final(tiles, outs, incoming, fields, totals)
    return (multipliers[None, None], residual[None, None])


def solution(mesh):
    in_specs = (
        P("cluster", "sub", None, None),
        P("cluster", "sub", None, None),
        P("sub", None, None),
        P("cluster", "sub", None),
        P("cluster", "sub", None),
        P("cluster", "sub", None, None),
    )
    out_specs = (P("cluster", "sub", None, None), P("cluster", "sub", None, None))
    return jax.shard_map(local, mesh=mesh, in_specs=in_specs, out_specs=out_specs, check_vma=False)
```

```python
import functools

import jax
import jax.numpy as jnp
from jax import lax
from jax.experimental import pallas as pl
from jax.experimental.pallas import tpu as pltpu
from jax.sharding import PartitionSpec as P

TILE = 128
MAXT = 4
RUNS = 4
NCOARSE = 128
EXTRA = 8
SCALE = 1.0 / 32.0
DISTANCES = (-2, -1, 1, 2)

VMEM = pl.BlockSpec(memory_space=pltpu.VMEM)
SMEM = pl.BlockSpec(memory_space=pltpu.SMEM)
HBM = pl.BlockSpec(memory_space=pltpu.HBM)
F32 = jnp.float32
BF16 = jnp.bfloat16
CHUNK = 256
BLOCK = 512
AHEAD = 2


def in_hbm(x):
    return pltpu.with_memory_space_constraint(x, pltpu.HBM)


def params(mebibytes):
    return pltpu.CompilerParams(vmem_limit_bytes=mebibytes * 1024 * 1024)


def halves(x):
    high = x.astype(BF16)
    low = (x - high.astype(F32)).astype(BF16)
    return high, low


def dot(a, b):
    return jnp.dot(a, b, preferred_element_type=F32)


def column_sum(x):
    return jnp.sum(x, axis=0, keepdims=True)


def run_starts(tiles):
    starts = [0]
    for k in range(RUNS):
        starts.append(starts[-1] + tiles[k])
    return starts


def tile_rows(tile, count=1):
    return pl.ds(pl.multiple_of(tile * TILE, TILE), count * TILE)


def each_tile(tiles, rows, live, padding):
    starts = run_starts(tiles)
    for k in range(RUNS):
        for j in range(MAXT):
            @pl.when(j < tiles[k])
            def _(k=k, j=j):
                live(tile_rows(starts[k] + j), k, slice(j * TILE, (j + 1) * TILE))
    if padding is None:
        return
    for t in range(RUNS, rows // TILE):
        @pl.when(t >= starts[RUNS])
        def _(t=t):
            padding(slice(t * TILE, (t + 1) * TILE))


class Pieces:
    def __init__(self, source, target, sems, first=0, size=CHUNK):
        self.copies = []
        for i in range(source.shape[0] // size):
            where = slice(i * size, (i + 1) * size)
            self.copies.append(
                pltpu.make_async_copy(source.at[where, :], target.at[where, :], sems.at[first + i])
            )

    def start(self):
        for copy in self.copies:
            copy.start()

    def wait(self):
        for copy in self.copies:
            copy.wait()


def gap_kernel(tiles_hbm, gap_hbm, o0, o1, o2, o3, tiles, gap, sem_tiles, sems):
    arrival = scalar_copy(tiles_hbm, tiles, sem_tiles)
    fetch = Pieces(gap_hbm, gap, sems, size=2 * CHUNK)
    fetch.start()
    arrival.wait()
    fetch.wait()
    starts = run_starts(tiles)
    for k, out in enumerate((o0, o1, o2, o3)):
        for j in range(MAXT):
            out[j * TILE:(j + 1) * TILE, :] = gap[tile_rows(starts[k] + j), :]


def gap_runs(tiles, gap):
    run = jax.ShapeDtypeStruct((MAXT * TILE, gap.shape[1]), F32)
    return pl.pallas_call(
        gap_kernel, out_shape=(run,) * RUNS, in_specs=[HBM, HBM], out_specs=(VMEM,) * RUNS,
        scratch_shapes=[
            pltpu.SMEM((RUNS,), jnp.int32), pltpu.VMEM(gap.shape, F32),
            pltpu.SemaphoreType.DMA(()), pltpu.SemaphoreType.DMA((RUNS,)),
        ],
        compiler_params=params(4), name="gap_runs",
    )(in_hbm(tiles), gap)


def prepare_kernel(tiles, coupling, corner_map, pair, turned, own_map, tiles_out, table):
    for k in range(RUNS):
        tiles_out[k] = tiles[k]
    table[...] = jnp.zeros(table.shape, jnp.int32)
    for k in range(RUNS):
        table[k:k + 1, :] = jnp.full((1, table.shape[1]), tiles[k], jnp.int32)
    corners, rows = coupling.shape
    high, low = halves(coupling[...])
    pair[0:corners, :] = high
    pair[corners:2 * corners, :] = low
    depth = turned.shape[1]
    for t in range(rows // TILE):
        block = coupling[:, t * TILE:(t + 1) * TILE]
        top = block.astype(BF16).astype(F32)
        rest = jnp.zeros((depth - 2 * corners, TILE), F32)
        stack = jnp.concatenate([top, block - top, rest], axis=0)
        turned[t * TILE:(t + 1) * TILE, :] = stack.T.astype(BF16)
    own_map[...] = jnp.zeros(own_map.shape, F32)
    own_map[0:1, 0:corners] = corner_map[...].astype(F32)


def prepare(tiles, coupling, corner_map, loads):
    corners, rows = coupling.shape
    return pl.pallas_call(
        prepare_kernel,
        out_shape=(
            jax.ShapeDtypeStruct((2 * corners, rows), BF16),
            jax.ShapeDtypeStruct((rows, TILE), BF16),
            jax.ShapeDtypeStruct((EXTRA, loads), F32),
            jax.ShapeDtypeStruct((RUNS,), jnp.int32),
            jax.ShapeDtypeStruct((EXTRA, loads), jnp.int32),
        ),
        in_specs=[SMEM, VMEM, VMEM],
        out_specs=(VMEM, VMEM, VMEM, SMEM, VMEM),
        compiler_params=params(8),
        cost_estimate=pl.CostEstimate(flops=10**6, bytes_accessed=8 * 10**6, transcendentals=0),
        name="prepare",
    )(tiles, coupling, corner_map)


def build_field(table, outs, incoming, field, split):
    tiles = [table[k, 0] for k in range(RUNS)]

    def live(where, k, block):
        x = outs[k][block, :] + incoming[k][block, :]
        field[where, :] = x
        high, low = halves(x)
        split[where, 0:TILE] = high
        split[where, TILE:2 * TILE] = low

    def padding(where):
        field[where, :] = jnp.zeros((TILE, field.shape[1]), F32)
        split[where, :] = jnp.zeros((TILE, split.shape[1]), BF16)

    each_tile(tiles, field.shape[0], live, padding)


def corner_values(pair, split):
    product = dot(pair[...], split[...])
    corners = pair.shape[0] // 2
    return (product[:corners, :TILE] + product[corners:, :TILE]) + (
        product[:corners, TILE:] + product[corners:, TILE:]
    )


def spread(values, payload, sems):
    copies = [
        pltpu.make_async_copy(values, payload.at[peer], sems.at[peer]) for peer in range(payload.shape[0])
    ]
    for copy in copies:
        copy.start()
    return copies


def assemble_kernel(first, tiles, o0, o1, o2, o3, i0, i1, i2, i3, pair, *rest):
    if first:
        extra, field_hbm, payload, field, split, values, sem_out, sems = rest
    else:
        field_hbm, payload, field, split, values, sem_out, sems = rest
    build_field(tiles, (o0, o1, o2, o3), (i0, i1, i2, i3), field, split)
    keep = Pieces(field, field_hbm, sem_out, size=2 * CHUNK)
    keep.start()
    corners = pair.shape[0] // 2
    values[0:corners, :] = corner_values(pair, split)
    if first:
        values[corners:, :] = extra[...]
    copies = spread(values, payload, sems)
    for copy in copies:
        copy.wait()
    keep.wait()


def assemble(first, tiles, outs, incoming, pair, extra, rows, peers):
    loads = outs[0].shape[1]
    corners = pair.shape[0] // 2
    depth = corners + (EXTRA if first else 0)
    more = (extra,) if first else ()
    return pl.pallas_call(
        functools.partial(assemble_kernel, first),
        out_shape=(pltpu.HBM((rows, loads), F32), pltpu.HBM((peers, depth, loads), F32)),
        in_specs=[VMEM] * (2 * RUNS + 2 + len(more)),
        out_specs=(HBM, HBM),
        scratch_shapes=[
            pltpu.VMEM((rows, loads), F32),
            pltpu.VMEM((rows, 2 * loads), BF16),
            pltpu.VMEM((depth, loads), F32),
            pltpu.SemaphoreType.DMA((rows // CHUNK,)),
            pltpu.SemaphoreType.DMA((peers,)),
        ],
        compiler_params=params(6),
        name="assemble_first" if first else "assemble",
    )(tiles, *outs, *incoming, pair, *more)


def operator_copy(operator_hbm, operator, sems, i):
    where = pl.ds(pl.multiple_of(i * CHUNK, CHUNK), CHUNK)
    return pltpu.make_async_copy(operator_hbm.at[where, :], operator.at[where, :], sems.at[i])


def local_kernel(step, operator_hbm, field_hbm, *rest):
    if step == 0:
        out, moments, operator, field, split, sem_field, sems = rest
    else:
        previous_hbm, old, out, moments, operator, field, split, previous, sem_field, sems, sem_previous = rest
    fetch = pltpu.make_async_copy(field_hbm, field, sem_field)
    fetch.start()
    rows, loads = out.shape
    count = rows // BLOCK

    def piece(i):
        where = pl.ds(pl.multiple_of(i * BLOCK, BLOCK), BLOCK)
        return pltpu.make_async_copy(operator_hbm.at[where, :], operator.at[where, :], sems.at[i])

    for i in range(AHEAD):
        piece(i).start()
    if step > 0:
        fetch_previous = pltpu.make_async_copy(previous_hbm, previous, sem_previous)
    fetch.wait()
    square = cross = jnp.zeros((1, loads), F32)
    for i in range(rows // CHUNK):
        where = slice(i * CHUNK, (i + 1) * CHUNK)
        x = field[where, :]
        high, low = halves(x)
        split[where, 0:TILE] = high
        split[where, TILE:2 * TILE] = low
        square = square + column_sum(x * x)
    def body(i, carry):
        piece(i).wait()

        @pl.when(i + AHEAD < count)
        def _():
            piece(i + AHEAD).start()

        if step > 0:
            @pl.when(i + AHEAD == count)
            def _():
                fetch_previous.start()

        where = pl.ds(pl.multiple_of(i * BLOCK, BLOCK), BLOCK)
        product = dot(operator[where, :], split[...])
        out[where, :] = product[:, :loads] + product[:, loads:]
        return carry

    lax.fori_loop(0, count, body, 0)
    if step > 0:
        fetch_previous.wait()
        cross = column_sum(field[...] * previous[...])
    if step == 0:
        moments[...] = jnp.zeros(moments.shape, F32)
        moments[0:1, :] = square
    else:
        moments[...] = old[...]
        moments[1:2, :] = cross
        moments[2:3, :] = square


def product_cost(rows, loads):
    return pl.CostEstimate(
        flops=4 * rows * rows * loads, bytes_accessed=2 * rows * rows + 8 * rows * loads, transcendentals=0
    )


def local_product(step, operator, field, previous=None, moments=None):
    rows, loads = field.shape
    pieces, single = pltpu.SemaphoreType.DMA((rows // CHUNK,)), pltpu.SemaphoreType.DMA(())
    more, more_specs, more_scratch, more_sems = (), [], [], []
    if step > 0:
        more, more_specs = (in_hbm(previous), moments), [HBM, VMEM]
        more_scratch, more_sems = [pltpu.VMEM((rows, loads), F32)], [single]
    return pl.pallas_call(
        functools.partial(local_kernel, step),
        out_shape=(jax.ShapeDtypeStruct((rows, loads), F32), jax.ShapeDtypeStruct((EXTRA, loads), F32)),
        in_specs=[HBM, HBM] + more_specs,
        out_specs=(VMEM, VMEM),
        scratch_shapes=[
            pltpu.VMEM(operator.shape, BF16),
            pltpu.VMEM((rows, loads), F32),
            pltpu.VMEM((rows, 2 * loads), BF16),
            *more_scratch,
            single,
            pieces,
            *more_sems,
        ],
        compiler_params=params(16),
        cost_estimate=product_cost(rows, loads),
        name=f"local_product{step}",
    )(operator, in_hbm(field), *more)


def load_kernel(operator_hbm, token, operator, sem):
    del token
    fetch = pltpu.make_async_copy(operator_hbm, operator, sem)
    fetch.start()
    fetch.wait()


def load_operator(operator, token):
    return pl.pallas_call(
        load_kernel, out_shape=pltpu.VMEM(operator.shape, BF16), in_specs=[HBM, HBM], out_specs=VMEM,
        scratch_shapes=[pltpu.SemaphoreType.DMA(())],
        compiler_params=params(2), cost_estimate=product_cost(operator.shape[0], TILE), name="load_operator",
    )(operator, token)


def joint_kernel(
    tiles, o0, o1, o2, o3, i0, i1, i2, i3, pair, operator, previous_hbm, old,
    field, payload, out, split, previous, sem_previous,
):
    fetch_previous = Pieces(previous_hbm, previous, sem_previous)
    fetch_previous.start()
    build_field(tiles, (o0, o1, o2, o3), (i0, i1, i2, i3), field, split)
    corners = pair.shape[0] // 2
    loads = out.shape[1]
    values = corner_values(pair, split)
    for peer in range(payload.shape[0]):
        payload[peer, 0:corners, :] = values
    fetch_previous.wait()
    zero = jnp.zeros((1, loads), F32)

    def body(i, totals):
        where = pl.ds(pl.multiple_of(i * BLOCK, BLOCK), BLOCK)
        product = dot(operator[where, :], split[...])
        value = product[:, :loads] + product[:, loads:]
        out[where, :] = value
        x = field[where, :]
        return (
            totals[0] + column_sum(x * previous[where, :]),
            totals[1] + column_sum(x * x),
            totals[2] + column_sum(x * value),
        )

    cross, square, local_sum = lax.fori_loop(0, out.shape[0] // BLOCK, body, (zero, zero, zero))
    row = lax.broadcasted_iota(jnp.int32, old.shape, 0)
    sums = old[...]
    for index, value in ((3, cross), (4, square), (5, local_sum)):
        sums = jnp.where(row == index, value, sums)
    for peer in range(payload.shape[0]):
        payload[peer, corners:, :] = sums


def joint(tiles, outs, incoming, pair, operator, previous, moments, peers):
    rows, loads = previous.shape
    depth = pair.shape[0] // 2 + EXTRA
    return pl.pallas_call(
        joint_kernel,
        out_shape=(
            jax.ShapeDtypeStruct((rows, loads), F32),
            jax.ShapeDtypeStruct((peers, depth, loads), F32),
            jax.ShapeDtypeStruct((rows, loads), F32),
        ),
        in_specs=[VMEM] * (2 * RUNS + 3) + [HBM, VMEM],
        out_specs=(VMEM, VMEM, VMEM),
        scratch_shapes=[
            pltpu.VMEM((rows, 2 * loads), BF16),
            pltpu.VMEM((rows, loads), F32),
            pltpu.SemaphoreType.DMA((rows // CHUNK,)),
        ],
        compiler_params=params(8),
        cost_estimate=product_cost(rows, loads),
        name="joint",
    )(tiles, *outs, *incoming, pair, operator, previous, moments)


def stacked(x):
    high, low = halves(x)
    row = jnp.concatenate([high, low], axis=1)
    return jnp.concatenate([row, row], axis=0)


def coarse_solve(gathered, maps, own_map, inverse, corners):
    loads = gathered.shape[2]
    index = lax.broadcasted_iota(jnp.int32, (NCOARSE, corners), 0).astype(F32)
    load = jnp.zeros((NCOARSE, 2 * loads), F32)
    for peer in range(gathered.shape[0]):
        choose = (index == maps[peer, 0:1, :corners]).astype(BF16)
        high, low = halves(gathered[peer, 0:corners, :])
        load = load + dot(choose, jnp.concatenate([high, low], axis=1))
    load = load[:, :loads] + load[:, loads:]
    high, low = halves(inverse[...])
    solved = dot(jnp.concatenate([high, low], axis=1), stacked(load))
    solved = solved[:, :loads] + solved[:, loads:]
    choose = (index == own_map[0:1, :corners]).astype(BF16)
    high, low = halves(solved)
    back = lax.dot_general(
        choose, jnp.concatenate([high, low], axis=1), (((0,), (0,)), ((), ())), preferred_element_type=F32
    )
    return load, solved, back[:, :loads] + back[:, loads:]


def scalar_copy(source, tiles, sem):
    copy = pltpu.make_async_copy(source, tiles, sem)
    copy.start()
    return copy


TILE_SCRATCH = [pltpu.SMEM((RUNS,), jnp.int32), pltpu.SemaphoreType.DMA(())]


def spread_back(tiles, arrival, back, local_part, turned, product, outs):
    corners, loads = back.shape
    rest = jnp.zeros((turned.shape[1] - 2 * corners, 2 * loads), BF16)
    wide = dot(turned[...], jnp.concatenate([stacked(back), rest], axis=0))
    product[...] = wide[:, :loads] + wide[:, loads:]
    arrival.wait()

    def live(where, k, block):
        outs[k][block, :] = (local_part[where, :] + product[where, :]) * SCALE

    each_tile(tiles, product.shape[0], live, None)


def coarse_kernel(step, corners, tiles_in, gathered, inverse, own_map, local_part, turned, *rest):
    *rest, tiles, sem = rest
    arrival = scalar_copy(tiles_in, tiles, sem)
    if step == 0:
        o0, o1, o2, o3, maps, product = rest
        for peer in range(gathered.shape[0]):
            maps[peer] = gathered[peer, corners:corners + EXTRA, :]
    else:
        maps, o0, o1, o2, o3, product = rest
    back = coarse_solve(gathered, maps, own_map, inverse, corners)[2]
    spread_back(tiles, arrival, back, local_part, turned, product, (o0, o1, o2, o3))


def coarse(step, corners, tiles, gathered, own_map, inverse, local_part, turned, maps):
    rows, loads = local_part.shape
    peers = gathered.shape[0]
    out_shape = [jax.ShapeDtypeStruct((MAXT * TILE, loads), F32)] * RUNS
    more = () if step == 0 else (maps,)
    if step == 0:
        out_shape.append(jax.ShapeDtypeStruct((peers, EXTRA, loads), F32))
    return pl.pallas_call(
        functools.partial(coarse_kernel, step, corners),
        out_shape=tuple(out_shape),
        in_specs=[VMEM] * (6 + len(more)),
        out_specs=(VMEM,) * len(out_shape),
        scratch_shapes=[pltpu.VMEM((rows, loads), F32)] + TILE_SCRATCH,
        compiler_params=params(6),
        name=f"coarse{step}",
    )(tiles, gathered, inverse, own_map, local_part, turned, *more)


def last_solve_kernel(corners, gathered, inverse, own_map, maps, back, sums_hbm, sums, sems):
    load, solved, value = coarse_solve(gathered, maps, own_map, inverse, corners)
    total = gathered[0, corners:corners + EXTRA, :]
    for peer in range(1, gathered.shape[0]):
        total = total + gathered[peer, corners:corners + EXTRA, :]
    row = lax.broadcasted_iota(jnp.int32, total.shape, 0)
    quad = column_sum(load * solved)
    total = jnp.where(row == 5, (total + quad) * (2.0 * SCALE), total)
    for peer in range(sums.shape[0]):
        sums[peer] = total
    keep = pltpu.make_async_copy(sums, sums_hbm, sems)
    keep.start()
    back[...] = value
    keep.wait()


def last_solve(corners, gathered, own_map, inverse, maps, sub_peers):
    loads = gathered.shape[2]
    return pl.pallas_call(
        functools.partial(last_solve_kernel, corners),
        out_shape=(jax.ShapeDtypeStruct((corners, loads), F32), pltpu.HBM((sub_peers, EXTRA, loads), F32)),
        in_specs=[VMEM] * 4, out_specs=(VMEM, HBM),
        scratch_shapes=[pltpu.VMEM((sub_peers, EXTRA, loads), F32), pltpu.SemaphoreType.DMA(())],
        compiler_params=params(4), name="last_solve",
    )(gathered, inverse, own_map, maps)


def last_spread_kernel(tiles_in, back, local_part, turned, o0, o1, o2, o3, product, tiles, sem):
    arrival = scalar_copy(tiles_in, tiles, sem)
    spread_back(tiles, arrival, back[...], local_part, turned, product, (o0, o1, o2, o3))


def last_spread(tiles, back, local_part, turned):
    rows, loads = local_part.shape
    return pl.pallas_call(
        last_spread_kernel,
        out_shape=(jax.ShapeDtypeStruct((MAXT * TILE, loads), F32),) * RUNS,
        in_specs=[VMEM] * 4, out_specs=(VMEM,) * RUNS,
        scratch_shapes=[pltpu.VMEM((rows, loads), F32)] + TILE_SCRATCH,
        compiler_params=params(6), cost_estimate=product_cost(rows // 2, loads), name="last_spread",
    )(tiles, back, local_part, turned)


def inner(m, p, q, lift):
    total = None
    for i in range(len(p)):
        for j in range(len(q)):
            term = p[i] * q[j] * m[i + j + lift]
            total = term if total is None else total + term
    return total


def coefficients(m):
    one = jnp.ones_like(m[0])
    res, dire, mult = [one], [one], []
    norm = m[0]
    for step in range(3):
        size = norm / inner(m, dire, dire, 1)
        mult = [
            (mult[i] if i < len(mult) else 0.0) + size * dire[i] for i in range(len(dire))
        ]
        grown = []
        for i in range(len(dire) + 1):
            value = res[i] if i < len(res) else jnp.zeros_like(one)
            grown.append(value - size * dire[i - 1] if i > 0 else value)
        res = grown
        if step < 2:
            fresh = inner(m, res, res, 0)
            ratio = fresh / norm
            dire = [res[i] + ratio * dire[i] if i < len(dire) else res[i] for i in range(len(res))]
            norm = fresh
    return mult, res


def final_kernel(
    tiles_in, o0, o1, o2, o3, i0, i1, i2, i3, v0, v1, v2, gathered, mult_hbm, res_hbm,
    out_mult, out_res, tiles, sem_tiles, sems
):
    arrival = scalar_copy(tiles_in, tiles, sem_tiles)
    outs, incoming = (o0, o1, o2, o3), (i0, i1, i2, i3)
    total = gathered[0]
    for peer in range(1, gathered.shape[0]):
        total = total + gathered[peer]
    mult, res = coefficients([total[i:i + 1, :] for i in range(6)])
    mult = [c * SCALE for c in mult]
    arrival.wait()
    rows = out_mult.shape[0]
    count = rows // TILE

    def leave(where, slot):
        for which, (source, target) in enumerate(((out_mult, mult_hbm), (out_res, res_hbm))):
            pltpu.make_async_copy(
                source.at[where, :], target.at[where, :], sems.at[which * count + slot]
            ).start()

    def live(where, k, block):
        a, b, c = v0[where, :], v1[where, :], v2[where, :]
        d = outs[k][block, :] + incoming[k][block, :]
        out_mult[where, :] = a * mult[0] + b * mult[1] + c * mult[2]
        out_res[where, :] = a * res[0] + b * res[1] + c * res[2] + d * res[3]
        leave(where, where.start // TILE)

    def padding(where):
        zero = jnp.zeros((TILE, out_mult.shape[1]), F32)
        out_mult[where, :] = zero
        out_res[where, :] = zero
        leave(where, where.start // TILE)

    each_tile(tiles, rows, live, padding)
    for which, (source, target) in enumerate(((out_mult, mult_hbm), (out_res, res_hbm))):
        for slot in range(count):
            where = slice(slot * TILE, (slot + 1) * TILE)
            pltpu.make_async_copy(
                source.at[where, :], target.at[where, :], sems.at[which * count + slot]
            ).wait()


def final(tiles, outs, incoming, fields, totals):
    rows, loads = fields[0].shape
    return pl.pallas_call(
        final_kernel, out_shape=(jax.ShapeDtypeStruct((rows, loads), F32),) * 2,
        in_specs=[VMEM] * (2 * RUNS + 5),
        out_specs=(HBM, HBM),
        scratch_shapes=[
            pltpu.VMEM((rows, loads), F32), pltpu.VMEM((rows, loads), F32), *TILE_SCRATCH,
            pltpu.SemaphoreType.DMA((2 * rows // TILE,)),
        ],
        compiler_params=params(6), name="final",
    )(tiles, *outs, *incoming, *fields, totals)


def exchange(outs):
    size = lax.axis_size("sub")
    incoming = []
    for k, distance in enumerate(DISTANCES):
        route = [((i + distance) % size, i) for i in range(size)]
        incoming.append(lax.ppermute(outs[RUNS - 1 - k], "sub", route))
    return incoming


def swap(blocks, axis):
    return lax.all_to_all(blocks, axis, 0, 0)


def local(dual_ops, corner_coupling, coarse_inverse, corner_map, interface_tiles, gap_terms):
    operator = in_hbm(dual_ops[0, 0])
    inverse = coarse_inverse[0]
    tiles = interface_tiles[0, 0]
    gap = in_hbm(gap_terms[0, 0])
    rows, loads = gap.shape
    corners = corner_map.shape[-1]
    peers = lax.axis_size("cluster")
    sub_peers = lax.axis_size("sub")

    outs = gap_runs(tiles, gap)
    incoming = exchange(outs)
    pair, turned, own_map, tiles, table = prepare(tiles, corner_coupling[0, 0], corner_map[0], loads)

    fields, moments, maps = [], None, None
    for step in range(3):
        if step < 2:
            field, payload = assemble(step == 0, table, outs, incoming, pair, own_map, rows, peers)
            gathered = swap(payload, "cluster")
            previous = fields[-1] if fields else None
            local_part, moments = local_product(step, operator, field, previous, moments)
        else:
            field, payload, local_part = joint(
                table, outs, incoming, pair, load_operator(operator, outs[0]), in_hbm(fields[-1]), moments, peers
            )
            gathered = swap(payload, "cluster")
        fields.append(field)
        if step < 2:
            outs = coarse(step, corners, tiles, gathered, own_map, inverse, local_part, turned, maps)
            if step == 0:
                outs, maps = outs[:RUNS], outs[RUNS]
        else:
            back, sums = last_solve(corners, gathered, own_map, inverse, maps, sub_peers)
            totals = swap(sums, "sub")
            outs = last_spread(tiles, back, local_part, turned)
        incoming = exchange(outs)
    multipliers, residual = final(tiles, outs, incoming, fields, totals)
    return (multipliers[None, None], residual[None, None])


def solution(mesh):
    in_specs = (
        P("cluster", "sub", None, None),
        P("cluster", "sub", None, None),
        P("sub", None, None),
        P("cluster", "sub", None),
        P("cluster", "sub", None),
        P("cluster", "sub", None, None),
    )
    out_specs = (P("cluster", "sub", None, None), P("cluster", "sub", None, None))
    return jax.shard_map(local, mesh=mesh, in_specs=in_specs, out_specs=out_specs, check_vma=False)
```

```python
import functools

import jax
import jax.numpy as jnp
from jax import lax
from jax.experimental import pallas as pl
from jax.experimental.pallas import tpu as pltpu
from jax.sharding import PartitionSpec as P

TILE = 128
MAXT = 4
RUNS = 4
NCOARSE = 128
EXTRA = 8
SCALE = 1.0 / 32.0
DISTANCES = (-2, -1, 1, 2)

VMEM = pl.BlockSpec(memory_space=pltpu.VMEM)
SMEM = pl.BlockSpec(memory_space=pltpu.SMEM)
HBM = pl.BlockSpec(memory_space=pltpu.HBM)
F32 = jnp.float32
BF16 = jnp.bfloat16
CHUNK = 256
BLOCK = 512
AHEAD = 2


def in_hbm(x):
    return pltpu.with_memory_space_constraint(x, pltpu.HBM)


def params(mebibytes):
    return pltpu.CompilerParams(vmem_limit_bytes=mebibytes * 1024 * 1024)


def halves(x):
    high = x.astype(BF16)
    low = (x - high.astype(F32)).astype(BF16)
    return high, low


def dot(a, b):
    return jnp.dot(a, b, preferred_element_type=F32)


def column_sum(x):
    return jnp.sum(x, axis=0, keepdims=True)


def run_starts(tiles):
    starts = [0]
    for k in range(RUNS):
        starts.append(starts[-1] + tiles[k])
    return starts


def tile_rows(tile, count=1):
    return pl.ds(pl.multiple_of(tile * TILE, TILE), count * TILE)


def each_tile(tiles, rows, live, padding):
    starts = run_starts(tiles)
    for k in range(RUNS):
        for j in range(MAXT):
            @pl.when(j < tiles[k])
            def _(k=k, j=j):
                live(tile_rows(starts[k] + j), k, slice(j * TILE, (j + 1) * TILE))
    if padding is None:
        return
    for t in range(RUNS, rows // TILE):
        @pl.when(t >= starts[RUNS])
        def _(t=t):
            padding(slice(t * TILE, (t + 1) * TILE))


class Pieces:
    def __init__(self, source, target, sems, first=0, size=CHUNK):
        self.copies = []
        for i in range(source.shape[0] // size):
            where = slice(i * size, (i + 1) * size)
            self.copies.append(
                pltpu.make_async_copy(source.at[where, :], target.at[where, :], sems.at[first + i])
            )

    def start(self):
        for copy in self.copies:
            copy.start()

    def wait(self):
        for copy in self.copies:
            copy.wait()


def gap_kernel(tiles_hbm, gap_hbm, o0, o1, o2, o3, tiles, gap, sem_tiles, sems):
    arrival = scalar_copy(tiles_hbm, tiles, sem_tiles)
    fetch = Pieces(gap_hbm, gap, sems, size=2 * CHUNK)
    fetch.start()
    arrival.wait()
    fetch.wait()
    starts = run_starts(tiles)
    for k, out in enumerate((o0, o1, o2, o3)):
        for j in range(MAXT):
            out[j * TILE:(j + 1) * TILE, :] = gap[tile_rows(starts[k] + j), :]


def gap_runs(tiles, gap):
    run = jax.ShapeDtypeStruct((MAXT * TILE, gap.shape[1]), F32)
    return pl.pallas_call(
        gap_kernel, out_shape=(run,) * RUNS, in_specs=[HBM, HBM], out_specs=(VMEM,) * RUNS,
        scratch_shapes=[
            pltpu.SMEM((RUNS,), jnp.int32), pltpu.VMEM(gap.shape, F32),
            pltpu.SemaphoreType.DMA(()), pltpu.SemaphoreType.DMA((RUNS,)),
        ],
        compiler_params=params(4), name="gap_runs",
    )(in_hbm(tiles), gap)


def prepare_kernel(tiles, coupling, corner_map, pair, turned, own_map, tiles_out, table):
    for k in range(RUNS):
        tiles_out[k] = tiles[k]
    table[...] = jnp.zeros(table.shape, jnp.int32)
    for k in range(RUNS):
        table[k:k + 1, :] = jnp.full((1, table.shape[1]), tiles[k], jnp.int32)
    corners, rows = coupling.shape
    high, low = halves(coupling[...])
    pair[0:corners, :] = high
    pair[corners:2 * corners, :] = low
    depth = turned.shape[1]
    for t in range(rows // TILE):
        block = coupling[:, t * TILE:(t + 1) * TILE]
        top = block.astype(BF16).astype(F32)
        rest = jnp.zeros((depth - 2 * corners, TILE), F32)
        stack = jnp.concatenate([top, block - top, rest], axis=0)
        turned[t * TILE:(t + 1) * TILE, :] = stack.T.astype(BF16)
    own_map[...] = jnp.zeros(own_map.shape, F32)
    own_map[0:1, 0:corners] = corner_map[...].astype(F32)


def prepare(tiles, coupling, corner_map, loads):
    corners, rows = coupling.shape
    return pl.pallas_call(
        prepare_kernel,
        out_shape=(
            jax.ShapeDtypeStruct((2 * corners, rows), BF16),
            jax.ShapeDtypeStruct((rows, TILE), BF16),
            jax.ShapeDtypeStruct((EXTRA, loads), F32),
            jax.ShapeDtypeStruct((RUNS,), jnp.int32),
            jax.ShapeDtypeStruct((EXTRA, loads), jnp.int32),
        ),
        in_specs=[SMEM, VMEM, VMEM],
        out_specs=(VMEM, VMEM, VMEM, SMEM, VMEM),
        compiler_params=params(8),
        cost_estimate=pl.CostEstimate(flops=10**6, bytes_accessed=8 * 10**6, transcendentals=0),
        name="prepare",
    )(tiles, coupling, corner_map)


def build_field(table, outs, incoming, field, split):
    tiles = [table[k, 0] for k in range(RUNS)]

    def live(where, k, block):
        x = outs[k][block, :] + incoming[k][block, :]
        field[where, :] = x
        high, low = halves(x)
        split[where, 0:TILE] = high
        split[where, TILE:2 * TILE] = low

    def padding(where):
        field[where, :] = jnp.zeros((TILE, field.shape[1]), F32)
        split[where, :] = jnp.zeros((TILE, split.shape[1]), BF16)

    each_tile(tiles, field.shape[0], live, padding)


def corner_values(pair, split):
    product = dot(pair[...], split[...])
    corners = pair.shape[0] // 2
    return (product[:corners, :TILE] + product[corners:, :TILE]) + (
        product[:corners, TILE:] + product[corners:, TILE:]
    )


def spread(values, payload, sems):
    copies = [
        pltpu.make_async_copy(values, payload.at[peer], sems.at[peer]) for peer in range(payload.shape[0])
    ]
    for copy in copies:
        copy.start()
    return copies


def assemble_kernel(first, tiles, o0, o1, o2, o3, i0, i1, i2, i3, pair, *rest):
    if first:
        extra, field_hbm, payload, field, split, values, sem_out, sems = rest
    else:
        field_hbm, payload, field, split, values, sem_out, sems = rest
    build_field(tiles, (o0, o1, o2, o3), (i0, i1, i2, i3), field, split)
    keep = Pieces(field, field_hbm, sem_out, size=2 * CHUNK)
    keep.start()
    corners = pair.shape[0] // 2
    values[0:corners, :] = corner_values(pair, split)
    if first:
        values[corners:, :] = extra[...]
    copies = spread(values, payload, sems)
    for copy in copies:
        copy.wait()
    keep.wait()


def assemble(first, tiles, outs, incoming, pair, extra, rows, peers):
    loads = outs[0].shape[1]
    corners = pair.shape[0] // 2
    depth = corners + (EXTRA if first else 0)
    more = (extra,) if first else ()
    return pl.pallas_call(
        functools.partial(assemble_kernel, first),
        out_shape=(pltpu.HBM((rows, loads), F32), pltpu.HBM((peers, depth, loads), F32)),
        in_specs=[VMEM] * (2 * RUNS + 2 + len(more)),
        out_specs=(HBM, HBM),
        scratch_shapes=[
            pltpu.VMEM((rows, loads), F32),
            pltpu.VMEM((rows, 2 * loads), BF16),
            pltpu.VMEM((depth, loads), F32),
            pltpu.SemaphoreType.DMA((rows // CHUNK,)),
            pltpu.SemaphoreType.DMA((peers,)),
        ],
        compiler_params=params(6),
        name="assemble_first" if first else "assemble",
    )(tiles, *outs, *incoming, pair, *more)


def operator_copy(operator_hbm, operator, sems, i):
    where = pl.ds(pl.multiple_of(i * CHUNK, CHUNK), CHUNK)
    return pltpu.make_async_copy(operator_hbm.at[where, :], operator.at[where, :], sems.at[i])


def local_kernel(step, operator_hbm, field_hbm, *rest):
    if step == 0:
        out, moments, operator, field, split, sem_field, sems = rest
    else:
        previous_hbm, old, out, moments, operator, field, split, previous, sem_field, sems, sem_previous = rest
    fetch = pltpu.make_async_copy(field_hbm, field, sem_field)
    fetch.start()
    rows, loads = out.shape
    count = rows // BLOCK

    def piece(i):
        where = pl.ds(pl.multiple_of(i * BLOCK, BLOCK), BLOCK)
        return pltpu.make_async_copy(operator_hbm.at[where, :], operator.at[where, :], sems.at[i])

    for i in range(AHEAD):
        piece(i).start()
    if step > 0:
        fetch_previous = pltpu.make_async_copy(previous_hbm, previous, sem_previous)
    fetch.wait()
    square = cross = jnp.zeros((1, loads), F32)
    for i in range(rows // CHUNK):
        where = slice(i * CHUNK, (i + 1) * CHUNK)
        x = field[where, :]
        high, low = halves(x)
        split[where, 0:TILE] = high
        split[where, TILE:2 * TILE] = low
        square = square + column_sum(x * x)
    def body(i, carry):
        piece(i).wait()

        @pl.when(i + AHEAD < count)
        def _():
            piece(i + AHEAD).start()

        if step > 0:
            @pl.when(i + AHEAD == count)
            def _():
                fetch_previous.start()

        where = pl.ds(pl.multiple_of(i * BLOCK, BLOCK), BLOCK)
        product = dot(operator[where, :], split[...])
        out[where, :] = product[:, :loads] + product[:, loads:]
        return carry

    lax.fori_loop(0, count, body, 0)
    if step > 0:
        fetch_previous.wait()
        cross = column_sum(field[...] * previous[...])
    if step == 0:
        moments[...] = jnp.zeros(moments.shape, F32)
        moments[0:1, :] = square
    else:
        moments[...] = old[...]
        moments[1:2, :] = cross
        moments[2:3, :] = square


def product_cost(rows, loads):
    return pl.CostEstimate(
        flops=4 * rows * rows * loads, bytes_accessed=2 * rows * rows + 8 * rows * loads, transcendentals=0
    )


def local_product(step, operator, field, previous=None, moments=None):
    rows, loads = field.shape
    pieces, single = pltpu.SemaphoreType.DMA((rows // CHUNK,)), pltpu.SemaphoreType.DMA(())
    more, more_specs, more_scratch, more_sems = (), [], [], []
    if step > 0:
        more, more_specs = (in_hbm(previous), moments), [HBM, VMEM]
        more_scratch, more_sems = [pltpu.VMEM((rows, loads), F32)], [single]
    return pl.pallas_call(
        functools.partial(local_kernel, step),
        out_shape=(jax.ShapeDtypeStruct((rows, loads), F32), jax.ShapeDtypeStruct((EXTRA, loads), F32)),
        in_specs=[HBM, HBM] + more_specs,
        out_specs=(VMEM, VMEM),
        scratch_shapes=[
            pltpu.VMEM(operator.shape, BF16),
            pltpu.VMEM((rows, loads), F32),
            pltpu.VMEM((rows, 2 * loads), BF16),
            *more_scratch,
            single,
            pieces,
            *more_sems,
        ],
        compiler_params=params(16),
        cost_estimate=product_cost(rows, loads),
        name=f"local_product{step}",
    )(operator, in_hbm(field), *more)


def load_kernel(operator_hbm, token, operator, sem):
    del token
    fetch = pltpu.make_async_copy(operator_hbm, operator, sem)
    fetch.start()
    fetch.wait()


def load_operator(operator, token):
    return pl.pallas_call(
        load_kernel, out_shape=pltpu.VMEM(operator.shape, BF16), in_specs=[HBM, HBM], out_specs=VMEM,
        scratch_shapes=[pltpu.SemaphoreType.DMA(())],
        compiler_params=params(2), cost_estimate=product_cost(operator.shape[0], TILE), name="load_operator",
    )(operator, token)


def joint_kernel(
    tiles, o0, o1, o2, o3, i0, i1, i2, i3, pair, operator, previous_hbm, old,
    field, payload, out, split, previous, sem_previous,
):
    fetch_previous = Pieces(previous_hbm, previous, sem_previous)
    fetch_previous.start()
    build_field(tiles, (o0, o1, o2, o3), (i0, i1, i2, i3), field, split)
    corners = pair.shape[0] // 2
    loads = out.shape[1]
    values = corner_values(pair, split)
    for peer in range(payload.shape[0]):
        payload[peer, 0:corners, :] = values
    fetch_previous.wait()
    zero = jnp.zeros((1, loads), F32)

    def body(i, totals):
        where = pl.ds(pl.multiple_of(i * BLOCK, BLOCK), BLOCK)
        product = dot(operator[where, :], split[...])
        value = product[:, :loads] + product[:, loads:]
        out[where, :] = value
        x = field[where, :]
        return (
            totals[0] + column_sum(x * previous[where, :]),
            totals[1] + column_sum(x * x),
            totals[2] + column_sum(x * value),
        )

    cross, square, local_sum = lax.fori_loop(
        0, out.shape[0] // BLOCK, body, (zero, zero, zero), unroll=2
    )
    row = lax.broadcasted_iota(jnp.int32, old.shape, 0)
    sums = old[...]
    for index, value in ((3, cross), (4, square), (5, local_sum)):
        sums = jnp.where(row == index, value, sums)
    for peer in range(payload.shape[0]):
        payload[peer, corners:, :] = sums


def joint(tiles, outs, incoming, pair, operator, previous, moments, peers):
    rows, loads = previous.shape
    depth = pair.shape[0] // 2 + EXTRA
    return pl.pallas_call(
        joint_kernel,
        out_shape=(
            jax.ShapeDtypeStruct((rows, loads), F32),
            jax.ShapeDtypeStruct((peers, depth, loads), F32),
            jax.ShapeDtypeStruct((rows, loads), F32),
        ),
        in_specs=[VMEM] * (2 * RUNS + 3) + [HBM, VMEM],
        out_specs=(VMEM, VMEM, VMEM),
        scratch_shapes=[
            pltpu.VMEM((rows, 2 * loads), BF16),
            pltpu.VMEM((rows, loads), F32),
            pltpu.SemaphoreType.DMA((rows // CHUNK,)),
        ],
        compiler_params=params(8),
        cost_estimate=product_cost(rows, loads),
        name="joint",
    )(tiles, *outs, *incoming, pair, operator, previous, moments)


def stacked(x):
    high, low = halves(x)
    row = jnp.concatenate([high, low], axis=1)
    return jnp.concatenate([row, row], axis=0)


def coarse_solve(gathered, maps, own_map, inverse, corners):
    loads = gathered.shape[2]
    index = lax.broadcasted_iota(jnp.int32, (NCOARSE, corners), 0).astype(F32)
    load = jnp.zeros((NCOARSE, 2 * loads), F32)
    for peer in range(gathered.shape[0]):
        choose = (index == maps[peer, 0:1, :corners]).astype(BF16)
        high, low = halves(gathered[peer, 0:corners, :])
        load = load + dot(choose, jnp.concatenate([high, low], axis=1))
    load = load[:, :loads] + load[:, loads:]
    high, low = halves(inverse[...])
    solved = dot(jnp.concatenate([high, low], axis=1), stacked(load))
    solved = solved[:, :loads] + solved[:, loads:]
    choose = (index == own_map[0:1, :corners]).astype(BF16)
    high, low = halves(solved)
    back = lax.dot_general(
        choose, jnp.concatenate([high, low], axis=1), (((0,), (0,)), ((), ())), preferred_element_type=F32
    )
    return load, solved, back[:, :loads] + back[:, loads:]


def scalar_copy(source, tiles, sem):
    copy = pltpu.make_async_copy(source, tiles, sem)
    copy.start()
    return copy


TILE_SCRATCH = [pltpu.SMEM((RUNS,), jnp.int32), pltpu.SemaphoreType.DMA(())]


def spread_back(tiles, arrival, back, local_part, turned, product, outs):
    corners, loads = back.shape
    rest = jnp.zeros((turned.shape[1] - 2 * corners, 2 * loads), BF16)
    wide = dot(turned[...], jnp.concatenate([stacked(back), rest], axis=0))
    product[...] = wide[:, :loads] + wide[:, loads:]
    arrival.wait()

    def live(where, k, block):
        outs[k][block, :] = (local_part[where, :] + product[where, :]) * SCALE

    each_tile(tiles, product.shape[0], live, None)


def coarse_kernel(step, corners, tiles_in, gathered, inverse, own_map, local_part, turned, *rest):
    *rest, tiles, sem = rest
    arrival = scalar_copy(tiles_in, tiles, sem)
    if step == 0:
        o0, o1, o2, o3, maps, product = rest
        for peer in range(gathered.shape[0]):
            maps[peer] = gathered[peer, corners:corners + EXTRA, :]
    else:
        maps, o0, o1, o2, o3, product = rest
    back = coarse_solve(gathered, maps, own_map, inverse, corners)[2]
    spread_back(tiles, arrival, back, local_part, turned, product, (o0, o1, o2, o3))


def coarse(step, corners, tiles, gathered, own_map, inverse, local_part, turned, maps):
    rows, loads = local_part.shape
    peers = gathered.shape[0]
    out_shape = [jax.ShapeDtypeStruct((MAXT * TILE, loads), F32)] * RUNS
    more = () if step == 0 else (maps,)
    if step == 0:
        out_shape.append(jax.ShapeDtypeStruct((peers, EXTRA, loads), F32))
    return pl.pallas_call(
        functools.partial(coarse_kernel, step, corners),
        out_shape=tuple(out_shape),
        in_specs=[VMEM] * (6 + len(more)),
        out_specs=(VMEM,) * len(out_shape),
        scratch_shapes=[pltpu.VMEM((rows, loads), F32)] + TILE_SCRATCH,
        compiler_params=params(6),
        name=f"coarse{step}",
    )(tiles, gathered, inverse, own_map, local_part, turned, *more)


def last_solve_kernel(corners, gathered, inverse, own_map, maps, back, sums_hbm, sums, sems):
    load, solved, value = coarse_solve(gathered, maps, own_map, inverse, corners)
    total = gathered[0, corners:corners + EXTRA, :]
    for peer in range(1, gathered.shape[0]):
        total = total + gathered[peer, corners:corners + EXTRA, :]
    row = lax.broadcasted_iota(jnp.int32, total.shape, 0)
    quad = column_sum(load * solved)
    total = jnp.where(row == 5, (total + quad) * (2.0 * SCALE), total)
    for peer in range(sums.shape[0]):
        sums[peer] = total
    keep = pltpu.make_async_copy(sums, sums_hbm, sems)
    keep.start()
    back[...] = value
    keep.wait()


def last_solve(corners, gathered, own_map, inverse, maps, sub_peers):
    loads = gathered.shape[2]
    return pl.pallas_call(
        functools.partial(last_solve_kernel, corners),
        out_shape=(jax.ShapeDtypeStruct((corners, loads), F32), pltpu.HBM((sub_peers, EXTRA, loads), F32)),
        in_specs=[VMEM] * 4, out_specs=(VMEM, HBM),
        scratch_shapes=[pltpu.VMEM((sub_peers, EXTRA, loads), F32), pltpu.SemaphoreType.DMA(())],
        compiler_params=params(4), name="last_solve",
    )(gathered, inverse, own_map, maps)


def last_spread_kernel(tiles_in, back, local_part, turned, o0, o1, o2, o3, product, tiles, sem):
    arrival = scalar_copy(tiles_in, tiles, sem)
    spread_back(tiles, arrival, back[...], local_part, turned, product, (o0, o1, o2, o3))


def last_spread(tiles, back, local_part, turned):
    rows, loads = local_part.shape
    return pl.pallas_call(
        last_spread_kernel,
        out_shape=(jax.ShapeDtypeStruct((MAXT * TILE, loads), F32),) * RUNS,
        in_specs=[VMEM] * 4, out_specs=(VMEM,) * RUNS,
        scratch_shapes=[pltpu.VMEM((rows, loads), F32)] + TILE_SCRATCH,
        compiler_params=params(6), cost_estimate=product_cost(rows // 2, loads), name="last_spread",
    )(tiles, back, local_part, turned)


def inner(m, p, q, lift):
    total = None
    for i in range(len(p)):
        for j in range(len(q)):
            term = p[i] * q[j] * m[i + j + lift]
            total = term if total is None else total + term
    return total


def coefficients(m):
    one = jnp.ones_like(m[0])
    res, dire, mult = [one], [one], []
    norm = m[0]
    for step in range(3):
        size = norm / inner(m, dire, dire, 1)
        mult = [
            (mult[i] if i < len(mult) else 0.0) + size * dire[i] for i in range(len(dire))
        ]
        grown = []
        for i in range(len(dire) + 1):
            value = res[i] if i < len(res) else jnp.zeros_like(one)
            grown.append(value - size * dire[i - 1] if i > 0 else value)
        res = grown
        if step < 2:
            fresh = inner(m, res, res, 0)
            ratio = fresh / norm
            dire = [res[i] + ratio * dire[i] if i < len(dire) else res[i] for i in range(len(res))]
            norm = fresh
    return mult, res


def final_kernel(
    tiles_in, o0, o1, o2, o3, i0, i1, i2, i3, v0, v1, v2, gathered, mult_hbm, res_hbm,
    out_mult, out_res, tiles, sem_tiles, sems
):
    arrival = scalar_copy(tiles_in, tiles, sem_tiles)
    outs, incoming = (o0, o1, o2, o3), (i0, i1, i2, i3)
    total = gathered[0]
    for peer in range(1, gathered.shape[0]):
        total = total + gathered[peer]
    mult, res = coefficients([total[i:i + 1, :] for i in range(6)])
    mult = [c * SCALE for c in mult]
    arrival.wait()
    rows = out_mult.shape[0]
    count = rows // TILE

    def leave(where, slot):
        for which, (source, target) in enumerate(((out_mult, mult_hbm), (out_res, res_hbm))):
            pltpu.make_async_copy(
                source.at[where, :], target.at[where, :], sems.at[which * count + slot]
            ).start()

    def live(where, k, block):
        a, b, c = v0[where, :], v1[where, :], v2[where, :]
        d = outs[k][block, :] + incoming[k][block, :]
        out_mult[where, :] = a * mult[0] + b * mult[1] + c * mult[2]
        out_res[where, :] = a * res[0] + b * res[1] + c * res[2] + d * res[3]
        leave(where, where.start // TILE)

    def padding(where):
        zero = jnp.zeros((TILE, out_mult.shape[1]), F32)
        out_mult[where, :] = zero
        out_res[where, :] = zero
        leave(where, where.start // TILE)

    each_tile(tiles, rows, live, padding)
    for which, (source, target) in enumerate(((out_mult, mult_hbm), (out_res, res_hbm))):
        for slot in range(count):
            where = slice(slot * TILE, (slot + 1) * TILE)
            pltpu.make_async_copy(
                source.at[where, :], target.at[where, :], sems.at[which * count + slot]
            ).wait()


def final(tiles, outs, incoming, fields, totals):
    rows, loads = fields[0].shape
    return pl.pallas_call(
        final_kernel, out_shape=(jax.ShapeDtypeStruct((rows, loads), F32),) * 2,
        in_specs=[VMEM] * (2 * RUNS + 5),
        out_specs=(HBM, HBM),
        scratch_shapes=[
            pltpu.VMEM((rows, loads), F32), pltpu.VMEM((rows, loads), F32), *TILE_SCRATCH,
            pltpu.SemaphoreType.DMA((2 * rows // TILE,)),
        ],
        compiler_params=params(6), name="final",
    )(tiles, *outs, *incoming, *fields, totals)


def exchange(outs):
    size = lax.axis_size("sub")
    incoming = []
    for k, distance in enumerate(DISTANCES):
        route = [((i + distance) % size, i) for i in range(size)]
        incoming.append(lax.ppermute(outs[RUNS - 1 - k], "sub", route))
    return incoming


def swap(blocks, axis):
    return lax.all_to_all(blocks, axis, 0, 0)


def local(dual_ops, corner_coupling, coarse_inverse, corner_map, interface_tiles, gap_terms):
    operator = in_hbm(dual_ops[0, 0])
    inverse = coarse_inverse[0]
    tiles = interface_tiles[0, 0]
    gap = in_hbm(gap_terms[0, 0])
    rows, loads = gap.shape
    corners = corner_map.shape[-1]
    peers = lax.axis_size("cluster")
    sub_peers = lax.axis_size("sub")

    outs = gap_runs(tiles, gap)
    incoming = exchange(outs)
    pair, turned, own_map, tiles, table = prepare(tiles, corner_coupling[0, 0], corner_map[0], loads)

    fields, moments, maps = [], None, None
    for step in range(3):
        if step < 2:
            field, payload = assemble(step == 0, table, outs, incoming, pair, own_map, rows, peers)
            gathered = swap(payload, "cluster")
            previous = fields[-1] if fields else None
            local_part, moments = local_product(step, operator, field, previous, moments)
        else:
            field, payload, local_part = joint(
                table, outs, incoming, pair, load_operator(operator, outs[0]), in_hbm(fields[-1]), moments, peers
            )
            gathered = swap(payload, "cluster")
        fields.append(field)
        if step < 2:
            outs = coarse(step, corners, tiles, gathered, own_map, inverse, local_part, turned, maps)
            if step == 0:
                outs, maps = outs[:RUNS], outs[RUNS]
        else:
            back, sums = last_solve(corners, gathered, own_map, inverse, maps, sub_peers)
            totals = swap(sums, "sub")
            outs = last_spread(tiles, back, local_part, turned)
        incoming = exchange(outs)
    multipliers, residual = final(tiles, outs, incoming, fields, totals)
    return (multipliers[None, None], residual[None, None])


def solution(mesh):
    in_specs = (
        P("cluster", "sub", None, None),
        P("cluster", "sub", None, None),
        P("sub", None, None),
        P("cluster", "sub", None),
        P("cluster", "sub", None),
        P("cluster", "sub", None, None),
    )
    out_specs = (P("cluster", "sub", None, None), P("cluster", "sub", None, None))
    return jax.shard_map(local, mesh=mesh, in_specs=in_specs, out_specs=out_specs, check_vma=False)
```
